768 devices in a mesh: tm: 8 (over z_hi, x), row: 16 (over y, core), col: 6 (over z_lo).
Axes of the slice: x: 4, y: 8, z: 12 (z_hi: 2, z_lo: 6; z = z_hi * 6 + z_lo), core: 2. Of those that a mesh axis runs over, the one named last changes fastest.
Arguments:
- c_occ: float32 [1536, 1536], P(None, 'tm'), may hold values from -1 to 1
- c_vir: float32 [1536, 1536], P(None, 'tm'), may hold values from -1 to 1
- eps_occ: float32 [1536], P('tm'), may hold values from -1.6 to -0.05, as said below
- eps_vir: float32 [1536], P('tm'), may hold values from 0.05 to 1.6, as said below
- tau: float32 [8], replicated, may hold values from 0.03 to 10
- tweight: float32 [8], replicated, may hold values from 0.02 to 0.15
- omega: float32 [32], replicated, may hold values from 0.05 to 5
- coulomb: float32 [1536, 1536], replicated, may hold values from -2 to 2
Outputs:
- screened: float32 [32, 1536, 1536], P('tm', 'row', 'col')
The draws below stay inside these ranges and needn't reach their ends.
Inputs may be any that keep to these rules, and one draw needn't show every extreme that they name: `eps_occ`: ascending along the orbital index. `eps_vir`: ascending along the orbital index.
All inputs are finite; a program needn't handle non-finite values.
Results may differ from the reference program's by a relative error of at most 0.00005.
Values sent between devices are 32-bit elements; how exact they have to be, the bound alone decides.
A program may use at most 64 MiB of HBM per device.

```python
import math
import jax
import jax.numpy as jnp
from jax import lax

N = 1536
NOCC = 1536
NVIR = 1536
TIMES = 8
FREQS = 32


def draw_coulomb(key, part):
    key_off, key_diag = jax.random.split(jax.random.fold_in(key, 11))
    off = jax.random.truncated_normal(key_off, -4.0, 4.0, (N, N), jnp.float32)
    off = (off + off.T) * (0.35 / jnp.sqrt(jnp.float32(N)))
    diagonal = jax.random.uniform(key_diag, (N,), jnp.float32, 1.0, 2.0)
    eye = jnp.eye(N, dtype=jnp.float32)
    return off * (1.0 - eye) + eye * diagonal[None, :]


def window_orbitals(key, rows, width, salt):
    groups = 8
    key_sign, key_shape, key_amp, key_noise = jax.random.split(jax.random.fold_in(key, salt), 4)
    signs = (2 * jax.random.randint(key_sign, (rows, groups), 0, 2) - 1).astype(jnp.float32)
    shape_mag = jax.random.uniform(key_shape, (rows, groups), jnp.float32, 0.5, 1.5)
    amplitude = jax.random.uniform(key_amp, (width,), jnp.float32, 0.5, 1.5)
    noise = jax.random.truncated_normal(key_noise, -4.0, 4.0, (rows, width), jnp.float32)
    member = jnp.arange(width) * groups // width
    onehot = (member[None, :] == jnp.arange(groups)[:, None]).astype(jnp.float32)
    coherent = jnp.dot(signs * shape_mag, onehot) * amplitude[None, :]
    return (0.9 * coherent + 0.7 * noise) / jnp.sqrt(jnp.float32(width))


def energy_ladder(key, count, low, high, salt):
    key_gap = jax.random.fold_in(key, salt)
    gaps = jax.random.uniform(key_gap, (count,), jnp.float32, 0.25, 1.75)
    climb = jnp.cumsum(gaps) - gaps[0]
    values = low + (high - low) * climb / climb[-1]
    return jnp.clip(values, low, high)


def draw_c_occ(key, part):
    return window_orbitals(key, N, NOCC, 41)


def draw_c_vir(key, part):
    return window_orbitals(key, N, NVIR, 43)


def draw_eps_occ(key, part):
    return energy_ladder(key, NOCC, -1.6, -0.05, 51)


def draw_eps_vir(key, part):
    return energy_ladder(key, NVIR, 0.05, 1.6, 53)


def setup_inputs(seed: int = 0) -> dict:
    streams_of = jax.random.split(jax.random.key(seed), 9)
    c_occ = draw_c_occ(jax.random.fold_in(streams_of[8], 71), 0)
    c_vir = draw_c_vir(jax.random.fold_in(streams_of[8], 71), 0)
    eps_occ = draw_eps_occ(jax.random.fold_in(streams_of[8], 71), 0)
    eps_vir = draw_eps_vir(jax.random.fold_in(streams_of[8], 71), 0)
    tau = jnp.clip(jnp.exp(jax.random.uniform(streams_of[4], (TIMES,), jnp.float32, math.log(0.03), math.log(10.0))), 0.03, 10.0)
    tweight = jnp.clip(jnp.exp(jax.random.uniform(streams_of[5], (TIMES,), jnp.float32, math.log(0.02), math.log(0.15))), 0.02, 0.15)
    omega = jnp.clip(jnp.exp(jax.random.uniform(streams_of[6], (FREQS,), jnp.float32, math.log(0.05), math.log(5.0))), 0.05, 5.0)
    coulomb = draw_coulomb(jax.random.fold_in(streams_of[8], 71), 0)
    return dict(c_occ=c_occ, c_vir=c_vir, eps_occ=eps_occ, eps_vir=eps_vir, tau=tau, tweight=tweight, omega=omega, coulomb=coulomb)


HIGH = lax.Precision.HIGHEST


def green_pair(c_occ, c_vir, eps_occ, eps_vir, tau_point):
    factor_occ = jnp.exp(eps_occ * tau_point)
    factor_vir = jnp.exp(-eps_vir * tau_point)
    green_occ = jnp.dot(c_occ * factor_occ[None, :], c_occ.T, precision=HIGH, preferred_element_type=jnp.float32)
    green_vir = jnp.dot(c_vir * factor_vir[None, :], c_vir.T, precision=HIGH, preferred_element_type=jnp.float32)
    return -2.0 * green_occ * green_vir


def reference(c_occ, c_vir, eps_occ, eps_vir, tau, tweight, omega, coulomb):
    polar_time = lax.map(lambda point: green_pair(c_occ, c_vir, eps_occ, eps_vir, point), tau)
    gamma = tweight[None, :] * jnp.cos(omega[:, None] * tau[None, :])

    def per_freq(weights):
        polar = jnp.tensordot(weights, polar_time, axes=1, precision=HIGH)
        coupled = jnp.dot(coulomb, polar, precision=HIGH, preferred_element_type=jnp.float32)
        first = coulomb + jnp.dot(coupled, coulomb, precision=HIGH, preferred_element_type=jnp.float32)
        return jnp.dot(coupled, first, precision=HIGH, preferred_element_type=jnp.float32)

    return lax.map(per_freq, gamma)
```

```python
import jax
import jax.numpy as jnp
from jax import lax
from jax.experimental import pallas as pl
from jax.experimental.pallas import tpu as pltpu
from jax.sharding import Mesh
from jax.sharding import PartitionSpec as P

AXES = ("zh", "x", "y", "c", "zl")
MESH_ID = pl.DeviceIdType.MESH
F32, BF16 = jnp.float32, jnp.bfloat16


def halves(value):
    high = value.astype(BF16)
    return high, (value - high.astype(F32)).astype(BF16)


def dot(a, b):
    return lax.dot_general(a, b, (((1,), (0,)), ((), ())), preferred_element_type=F32)


def remote(src, dst, send, recv, device):
    return pltpu.make_async_remote_copy(
        src_ref=src, dst_ref=dst, send_sem=send, recv_sem=recv, device_id=device, device_id_type=MESH_ID
    )


def kernel(
    tau, gamma, eps_occ, eps_vir, occ, vir, coulomb, out,
    rows_t, left, part, half_in, from_side, z_out, z_in, times, freqs, blocks,
    p_high, p_low, v_full, v_high, v_low, first, stack_a, stack_b, tiles, landed,
    v_sem, x_send, x_recv, z_send, z_recv, a_send, a_self, a_recv,
    l_send, l_recv, y_send, y_recv, c_send, c_recv, o_send, o_recv,
):
    zh, x, y, c, zl = (lax.axis_index(a) for a in AXES)
    level = zl + zh * (5 - 2 * zl)
    own = level * 2 + c
    parity = lax.rem(y, 2)
    pair = lax.div(y, 2)
    x_right, x_left = lax.rem(x + 1, 4), lax.rem(x + 3, 4)
    other = 1 - zh

    def at(zh_=zh, x_=x, y_=y, c_=c, zl_=zl):
        return (zh_, x_, y_, c_, zl_)

    def line_of(zh_, level_):
        return level_ + zh_ * (5 - 2 * level_)

    load_v = pltpu.make_async_copy(coulomb, v_full, v_sem)
    load_v.start()

    barrier = pltpu.get_barrier_semaphore()

    def greet(device):
        pl.semaphore_signal(barrier, inc=1, device_id=device, device_id_type=MESH_ID)

    turn = 6 * (2 * parity + c) + zl + 6 * pair + 15
    strip = lax.rem(turn, 24)

    def tile_to(col, h):
        half = 2 * strip + h
        q = lax.div(half, 3)
        return q, lax.rem(half, 3), jnp.logical_and(q == 2 * y + c, col == zl)

    def tile_from(f, slot):
        r = lax.div(3 * (2 * y + c) + slot, 2)
        u = lax.rem(r + 48 - 15 - 6 * f, 24)
        pc, zl_s = lax.div(u, 6), lax.rem(u, 6)
        y_s, c_s = 2 * f + lax.div(pc, 2), lax.rem(pc, 2)
        same = jnp.logical_and(jnp.logical_and(y_s == y, c_s == c), zl_s == zl)
        return at(y_=y_s, c_=c_s, zl_=zl_s), same

    def freq_to(k):
        zh_k, x_k, f = lax.div(k, 16), lax.rem(lax.div(k, 4), 4), lax.rem(k, 4)
        y_k = 2 * f + lax.rem(x, 2)
        same = jnp.logical_and(jnp.logical_and(zh_k == zh, x_k == x), y_k == y)
        return (zh_k, x_k, y_k, c, line_of(zh_k, level)), same

    greet(at(x_=x_left))
    greet(at(x_=x_right))
    greet(at(zh_=other, zl_=5 - zl))
    greet(at(y_=y + 1 - 2 * parity))
    greet(at(c_=1 - c))

    @pl.when(zl > 0)
    def _():
        greet(at(zl_=zl - 1))

    @pl.when(zl < 5)
    def _():
        greet(at(zl_=zl + 1))

    def greet_source(n, carry):
        zh_s, x_s, y_s = lax.div(n, 16), 2 * lax.rem(lax.div(n, 8), 2) + parity, lax.rem(n, 8)
        same = jnp.logical_and(jnp.logical_and(zh_s == zh, x_s == x), y_s == y)

        @pl.when(jnp.logical_not(same))
        def _():
            greet((zh_s, x_s, y_s, c, line_of(zh_s, level)))

        return carry

    lax.fori_loop(0, 32, greet_source, 0)

    def greet_tile(n, carry):
        device, same = tile_from(lax.div(n, 3), lax.rem(n, 3))

        @pl.when(jnp.logical_not(same))
        def _():
            greet(device)

        return carry

    lax.fori_loop(0, 12, greet_tile, 0)

    for side, (block, eps, sign) in enumerate(((occ, eps_occ, 1.0), (vir, eps_vir, -1.0))):
        rows_t[...] = block[:, pl.ds(pl.multiple_of(own * 128, 128), 128)].T
        rows = rows_t[pl.ds(pl.multiple_of(y * 16, 16), 16), :]
        for t in range(8):
            high, low = halves(rows * jnp.exp(eps[...] * (sign * tau[t])))
            left[side, t * 16 : t * 16 + 16, :] = high
            left[side, 128 + t * 16 : 144 + t * 16, :] = low
    for d in (2, 1, 3, 0):
        for z in range(2):
            col = lax.rem(own + z * 4 + lax.rem(x + d, 4), 12)
            for side, block in enumerate((occ, vir)):
                high, low = halves(block[:, pl.ds(pl.multiple_of(col * 128, 128), 128)])
                both = dot(left[side], high)
                part[d, z, side * 128 : side * 128 + 128, :] = (
                    both[:128] + both[128:] + dot(left[side, :128, :], low)
                )

    is_self = jnp.logical_and(lax.rem(x, 2) == parity, True).astype(jnp.int32)
    tile_self = jnp.int32(0)
    for h in range(2):
        tile_self = tile_self + (tile_to(zl, h)[2]).astype(jnp.int32)
    inner = (zl > 0).astype(jnp.int32) + (zl < 5).astype(jnp.int32)
    pl.semaphore_wait(barrier, 5 + inner + 32 - is_self + 12 - tile_self)

    right_dev, left_dev = at(x_=x_right), at(x_=x_left)
    sends = [
        remote(part.at[2, 0], half_in.at[0], x_send.at[0], x_recv.at[0], right_dev),
        remote(part.at[2, 1], half_in.at[1], x_send.at[1], x_recv.at[1], left_dev),
        remote(part.at[1, 1], from_side.at[0, 1], x_send.at[2], x_recv.at[2], right_dev),
        remote(part.at[3, 0], from_side.at[1, 0], x_send.at[3], x_recv.at[3], left_dev),
        remote(part.at[1, 0], from_side.at[0, 0], x_send.at[4], x_recv.at[4], right_dev),
        remote(part.at[3, 1], from_side.at[1, 1], x_send.at[5], x_recv.at[5], left_dev),
    ]
    for n in range(4):
        sends[n].start()
    sends[0].wait_recv()
    part[1, 0] = part[1, 0] + half_in[0]
    sends[4].start()
    sends[1].wait_recv()
    part[3, 1] = part[3, 1] + half_in[1]
    sends[5].start()

    load_v.wait()

    def split_v(n, carry):
        rows = pl.ds(pl.multiple_of(n * 64, 64), 64)
        high, low = halves(v_full[rows, :])
        v_high[rows, :] = high
        v_low[rows, :] = low
        return carry

    lax.fori_loop(0, 24, split_v, 0)
    for n in range(2, 6):
        sends[n].wait_recv()

    z_out[...] = part[0, other] + from_side[0, other] + from_side[1, other]
    cross = remote(z_out, z_in, z_send, z_recv, at(zh_=other, zl_=5 - zl))
    cross.start()
    z_keep = part[0, zh] + from_side[0, zh] + from_side[1, zh]
    half_in[0] = z_keep
    cross.wait_recv()
    times[...] = -2.0 * (half_in[0, :128, :] + z_in[:128, :]) * (half_in[0, 128:, :] + z_in[128:, :])

    def one_freq(k, carry):
        total = gamma[k, 0] * times[0:16, :]
        for t in range(1, 8):
            total = total + gamma[k, t] * times[t * 16 : t * 16 + 16, :]
        freqs[k] = total
        return carry

    lax.fori_loop(0, 32, one_freq, 0)

    member = zh * 4 + x
    place = blocks.at[own, lax.rem(x, 2), lax.div(member, 2), pl.ds(pl.multiple_of(y * 16, 16), 16), :]
    mine = member * 4 + pair

    def send_freq(n, carry):
        k = lax.rem(mine + n, 32)
        device, _same = freq_to(k)
        remote(freqs.at[k], place, a_send, a_recv, device).start()
        return carry

    lax.fori_loop(1, 32, send_freq, 0)
    to_pair, same_pair = freq_to(mine)

    @pl.when(same_pair)
    def _():
        pltpu.make_async_copy(freqs.at[mine], place, a_recv).start()

    @pl.when(jnp.logical_not(same_pair))
    def _():
        remote(freqs.at[mine], place, a_self, a_recv, to_pair).start()

    own_block = blocks.at[own, parity]
    pltpu.make_async_copy(own_block, own_block, a_recv).wait()

    def needed(level_, par, m2):
        return jnp.logical_or(m2 < 3, jnp.logical_and(par == 0, level_ < 3))

    def expand(i, par, m2):
        m = 2 * m2 + par
        col = lax.rem(i + m, 12)
        here = pl.ds(pl.multiple_of(i * 128, 128), 128)
        there = pl.ds(pl.multiple_of(col * 128, 128), 128)
        value = blocks[i, par, m2]
        high, low = halves(value)
        p_high[here, there] = high
        p_low[here, there] = low

        @pl.when(m > 0)
        def _():
            high_t, low_t = halves(value.T)
            p_high[there, here] = high_t
            p_low[there, here] = low_t

    def line_copy(j, m2, side):
        ref = blocks.at[line_of(zh, j) * 2 + c, parity, m2]
        return remote(ref, ref, l_send.at[side, j * 4 + m2], l_recv.at[j * 4 + m2], at(zl_=zl + 1 - 2 * side))

    def y_copy(j, m2, par):
        ref = blocks.at[line_of(zh, j) * 2 + c, par, m2]
        return remote(ref, ref, y_send.at[j * 4 + m2], y_recv.at[j * 4 + m2], at(y_=y + 1 - 2 * parity))

    def c_copy(j, m2, par, core):
        ref = blocks.at[line_of(zh, j) * 2 + core, par, m2]
        n = par * 24 + j * 4 + m2
        return remote(ref, ref, c_send.at[n], c_recv.at[n], at(c_=1 - c))

    def from_line(j, m2, d, side):
        copy = line_copy(j, m2, side)

        @pl.when(d > 0)
        def _():
            copy.wait_recv()

        far = zl + 1 - 2 * side

        @pl.when(jnp.logical_and(far >= 0, far < 6))
        def _():
            copy.start()

        @pl.when(jnp.logical_or(d > 0, side == 0))
        def _():
            y_copy(j, m2, parity).start()
            c_copy(j, m2, parity, c).start()
            expand(line_of(zh, j) * 2 + c, parity, m2)

    def from_pair(j, m2):
        y_copy(j, m2, 1 - parity).wait_recv()
        c_copy(j, m2, 1 - parity, c).start()
        expand(line_of(zh, j) * 2 + c, 1 - parity, m2)

    def from_core(j, m2, par):
        c_copy(j, m2, par, 1 - c).wait_recv()
        expand(line_of(zh, j) * 2 + 1 - c, par, m2)

    def gather(n, carry):
        step, m2, side = lax.div(n, 8), lax.rem(lax.div(n, 2), 4), lax.rem(n, 2)

        def stage(lag, par, action, twice=False):
            d = step - lag
            j = zl - d * (1 - 2 * side)
            live = jnp.logical_and(jnp.logical_and(d >= 0, d < 6), jnp.logical_and(j >= 0, j < 6))
            if not twice:
                live = jnp.logical_and(live, jnp.logical_or(d > 0, side == 0))
            live = jnp.logical_and(live, needed(line_of(zh, j), par, m2))

            @pl.when(live)
            def _():
                action(j, d)

        stage(0, parity, lambda j, d: from_line(j, m2, d, side), True)
        stage(1, 1 - parity, lambda j, d: from_pair(j, m2))
        stage(1, parity, lambda j, d: from_core(j, m2, parity))
        stage(2, 1 - parity, lambda j, d: from_core(j, m2, 1 - parity))
        return carry

    lax.fori_loop(0, 64, gather, 0)

    rows = pl.ds(pl.multiple_of(strip * 64, 64), 64)
    stack_a[:64, :] = v_high[rows, :]
    stack_a[64:, :] = v_low[rows, :]

    def product(src, high, low, use):
        def step(n, carry):
            cols = pl.ds(pl.multiple_of(n * 256, 256), 256)
            both = dot(src[...], high[:, cols])
            use(n, cols, both[:64] + both[64:] + dot(src[:64, :], low[:, cols]))
            return carry

        lax.fori_loop(0, 6, step, 0)

    def keep(dst, cols, value):
        high, low = halves(value)
        dst[:64, cols] = high
        dst[64:, cols] = low

    def use_one(n, cols, value):
        first[:, cols] = value
        keep(stack_b, cols, value)

    def send_tile(n, cols, value):
        tiles[n] = value
        for h in range(2):
            q, slot, same = tile_to(n, h)
            src = tiles.at[n, pl.ds(32 * h, 32), :]
            dst = landed.at[pair, slot]

            @pl.when(same)
            def _():
                pltpu.make_async_copy(src, dst, o_recv).start()

            @pl.when(jnp.logical_not(same))
            def _():
                remote(src, dst, o_send.at[2 * n + h], o_recv, at(y_=lax.div(q, 2), c_=lax.rem(q, 2), zl_=n)).start()

    product(stack_a, p_high, p_low, use_one)
    product(stack_b, v_high, v_low, lambda n, cols, value: keep(stack_a, cols, value))
    product(stack_a, p_high, p_low, lambda n, cols, value: keep(stack_b, cols, first[:, cols] + value))
    product(stack_b, v_high, v_low, send_tile)

    pltpu.make_async_copy(landed, landed, o_recv).wait()
    out[...] = landed[...].reshape(out.shape)

    for n in range(6):
        sends[n].wait_send()
    cross.wait_send()
    pltpu.make_async_copy(freqs.at[pl.ds(0, 31)], freqs.at[pl.ds(0, 31)], a_send).wait()

    @pl.when(jnp.logical_not(same_pair))
    def _():
        pltpu.make_async_copy(freqs.at[0], freqs.at[0], a_self).wait()

    def drain(n, carry):
        j, m2 = lax.div(n, 4), lax.rem(n, 4)
        level_ = line_of(zh, j)

        @pl.when(needed(level_, parity, m2))
        def _():
            y_copy(j, m2, parity).wait_send()
            c_copy(j, m2, parity, c).wait_send()

            @pl.when(jnp.logical_and(j <= zl, zl < 5))
            def _():
                line_copy(j, m2, 0).wait_send()

            @pl.when(jnp.logical_and(j >= zl, zl > 0))
            def _():
                line_copy(j, m2, 1).wait_send()

        @pl.when(needed(level_, 1 - parity, m2))
        def _():
            c_copy(j, m2, 1 - parity, c).wait_send()

        return carry

    lax.fori_loop(0, 24, drain, 0)

    def drain_tiles(n, carry):
        col, h = lax.div(n, 2), lax.rem(n, 2)
        same = tile_to(col, h)[2]

        @pl.when(jnp.logical_not(same))
        def _():
            src = tiles.at[0, pl.ds(0, 32), :]
            pltpu.make_async_copy(src, src, o_send.at[n]).wait()

        return carry

    lax.fori_loop(0, 12, drain_tiles, 0)


def on_device(c_occ, c_vir, eps_occ, eps_vir, tau, tweight, omega, coulomb):
    gamma = tweight[None, :] * jnp.cos(omega[:, None] * tau[None, :])
    grid = coulomb.shape[0]
    width = c_occ.shape[1]
    dma = pltpu.SemaphoreType.DMA
    vmem, smem = pl.BlockSpec(memory_space=pltpu.VMEM), pl.BlockSpec(memory_space=pltpu.SMEM)
    return pl.pallas_call(
        kernel,
        out_shape=jax.ShapeDtypeStruct((4, 96, 256), F32),
        in_specs=[smem, smem, vmem, vmem, vmem, vmem, pl.BlockSpec(memory_space=pl.ANY)],
        out_specs=vmem,
        scratch_shapes=[
            pltpu.VMEM((128, width), F32),
            pltpu.VMEM((2, 256, width), BF16),
            pltpu.VMEM((4, 2, 256, 128), F32),
            pltpu.VMEM((2, 256, 128), F32),
            pltpu.VMEM((2, 2, 256, 128), F32),
            pltpu.VMEM((256, 128), F32),
            pltpu.VMEM((256, 128), F32),
            pltpu.VMEM((128, 128), F32),
            pltpu.VMEM((32, 16, 128), F32),
            pltpu.VMEM((12, 2, 4, 128, 128), F32),
            pltpu.VMEM((grid, grid), BF16),
            pltpu.VMEM((grid, grid), BF16),
            pltpu.VMEM((grid, grid), F32),
            pltpu.VMEM((grid, grid), BF16),
            pltpu.VMEM((grid, grid), BF16),
            pltpu.VMEM((64, grid), F32),
            pltpu.VMEM((128, grid), BF16),
            pltpu.VMEM((128, grid), BF16),
            pltpu.VMEM((6, 64, 256), F32),
            pltpu.VMEM((4, 3, 32, 256), F32),
            dma, dma((6,)), dma((6,)), dma, dma, dma, dma, dma,
            dma((2, 24)), dma((24,)), dma((24,)), dma((24,)), dma((48,)), dma((48,)), dma((12,)), dma,
        ],
        compiler_params=pltpu.CompilerParams(
            collective_id=0, has_side_effects=True, vmem_limit_bytes=60 * 1024 * 1024
        ),
        name="screened",
    )(tau, gamma, eps_occ[None, :], eps_vir[None, :], c_occ.T, c_vir.T, coulomb)


def solution(mesh):
    split = Mesh(mesh.devices.reshape(2, 4, 8, 2, 6), AXES)
    tm = ("zh", "x")
    placed = (P(None, tm), P(None, tm), P(tm), P(tm), P(), P(), P(), P())
    return jax.shard_map(
        on_device, mesh=split, in_specs=placed, out_specs=P(tm, ("y", "c"), "zl"), check_vma=False
    )
```

```python
import jax
import jax.numpy as jnp
from jax import lax
from jax.experimental import pallas as pl
from jax.experimental.pallas import tpu as pltpu
from jax.sharding import Mesh
from jax.sharding import PartitionSpec as P

AXES = ("zh", "x", "y", "c", "zl")
MESH_ID = pl.DeviceIdType.MESH
F32, BF16 = jnp.float32, jnp.bfloat16

BATCH = 4
SPREAD = ("xyz", "zxy", "zyx", "xyz")
PIECES = (
    (0, 0, 0, 0), (1, 0, 0, 0), (2, 0, 0, 0), (3, 0, 0, 0), (0, 0, 1, 0), (0, 0, 0, 1),
    (0, 1, 0, 0), (1, 1, 0, 0), (1, 0, 1, 0), (1, 0, 0, 1), (2, 1, 0, 0), (2, 0, 0, 1),
    (2, 0, 1, 0), (0, 2, 0, 0), (3, 0, 1, 0), (3, 0, 0, 1), (3, 1, 0, 0), (0, 0, 1, 1),
    (1, 1, 1, 0), (0, 1, 1, 0), (0, 1, 0, 1), (1, 2, 0, 0), (1, 1, 0, 1), (1, 0, 1, 1),
    (2, 1, 1, 0), (2, 0, 1, 1), (2, 2, 0, 0), (2, 1, 0, 1), (3, 2, 0, 0), (1, 2, 1, 0),
    (3, 1, 1, 0), (3, 1, 0, 1), (3, 0, 1, 1), (1, 2, 0, 1), (0, 2, 1, 0), (0, 2, 0, 1),
    (1, 1, 1, 1), (0, 1, 1, 1), (2, 2, 1, 0), (2, 1, 1, 1), (2, 2, 0, 1), (3, 2, 1, 0),
    (3, 2, 0, 1), (0, 2, 1, 1), (1, 2, 1, 1), (3, 1, 1, 1), (2, 2, 1, 1), (3, 2, 1, 1),
)


def halves(value):
    high = value.astype(BF16)
    return high, (value - high.astype(F32)).astype(BF16)


def dot(a, b):
    return lax.dot_general(a, b, (((1,), (0,)), ((), ())), preferred_element_type=F32)


def remote(src, dst, send, recv, device):
    return pltpu.make_async_remote_copy(
        src_ref=src, dst_ref=dst, send_sem=send, recv_sem=recv, device_id=device, device_id_type=MESH_ID
    )


def kernel(
    tau, tweight, omega, eps_occ, eps_vir, occ_in, vir_in, coulomb, out,
    rows_t, left, part, half_in, from_side, z_out, z_in, times, freqs, blocks,
    p_high, p_low, v_full, v_high, v_low, first, stack_a, stack_b, tiles, landed,
    tables, occ, vir, b_sem, v_sem, x_send, x_recv, z_send, z_recv, a_send, a_self, a_recv,
    g_send, g_recv, c_send, c_recv, o_send, o_recv,
):
    zh, x, y, c, zl = (lax.axis_index(a) for a in AXES)
    level = zl + zh * (5 - 2 * zl)
    own = level * 2 + c
    triple, bz = lax.div(level, 3), lax.rem(level, 3)
    x_pair, bx = lax.div(x, 2), lax.rem(x, 2)
    y_pair, by = lax.div(y, 2), lax.rem(y, 2)
    x_freq = 2 * x_pair + lax.rem(y_pair, 2)
    slot_freq = 2 * lax.div(y_pair, 2) + triple
    home = (by * 3 + bz) * 2 + c
    x_right, x_left = lax.rem(x + 1, 4), lax.rem(x + 3, 4)
    other = 1 - zh

    def at(zh_=zh, x_=x, y_=y, c_=c, zl_=zl):
        return (zh_, x_, y_, c_, zl_)

    def line_of(zh_, level_):
        return level_ + zh_ * (5 - 2 * level_)

    load_v = pltpu.make_async_copy(coulomb, v_full, v_sem)
    loads = [
        pltpu.make_async_copy(occ_in, occ, b_sem.at[0]),
        pltpu.make_async_copy(vir_in, vir, b_sem.at[1]),
    ]
    for load in loads:
        load.start()
    load_v.start()

    barrier = pltpu.get_barrier_semaphore()

    def greet(device):
        pl.semaphore_signal(barrier, inc=1, device_id=device, device_id_type=MESH_ID)

    strip = lax.rem(6 * (2 * by + bx) + c * 3 + bz + 6 * y_pair + 15, 24)

    def tile_to(col, h):
        half = 2 * strip + h
        q = lax.div(half, 3)
        same = jnp.logical_and(jnp.logical_and(q == 2 * y + c, col == zl), x_freq == x)
        return q, lax.rem(half, 3), same

    def tile_from(f, slot):
        y_pair_s = 2 * lax.div(f, 2) + bx
        r = lax.div(3 * (2 * y + c) + slot, 2)
        u = lax.rem(r + 81 - 6 * y_pair_s, 24)
        a, b = lax.div(u, 6), lax.rem(u, 6)
        x_s, y_s = 2 * x_pair + lax.rem(a, 2), 2 * y_pair_s + lax.div(a, 2)
        zl_s, c_s = line_of(zh, 3 * lax.rem(f, 2) + lax.rem(b, 3)), lax.div(b, 3)
        same = jnp.logical_and(
            jnp.logical_and(y_s == y, c_s == c), jnp.logical_and(zl_s == zl, x_s == x)
        )
        return at(x_=x_s, y_=y_s, c_=c_s, zl_=zl_s), same

    def freq_to(k):
        zh_k, x_k, f = lax.div(k, 16), lax.rem(lax.div(k, 4), 4), lax.rem(k, 4)
        x_d = 2 * lax.div(x_k, 2) + bx
        y_d = 2 * (2 * lax.div(f, 2) + lax.rem(x_k, 2)) + triple
        return (zh_k, x_d, y_d, c, line_of(zh_k, 3 * lax.rem(f, 2) + bz))

    greet(at(x_=x_left))
    greet(at(x_=x_right))
    greet(at(zh_=other, zl_=5 - zl))
    greet(at(y_=y + 1 - 2 * by))
    greet(at(c_=1 - c))

    def neighbour(step):
        return at(zl_=line_of(zh, level + step))

    @pl.when(bz > 0)
    def _():
        greet(neighbour(-1))

    @pl.when(bz < 2)
    def _():
        greet(neighbour(1))

    same_home = triple == by

    def greet_source(n, carry):
        zh_s, x_s, y_s = lax.div(n, 16), 2 * lax.rem(lax.div(n, 8), 2) + bx, lax.rem(n, 8)
        same = jnp.logical_and(jnp.logical_and(zh_s == zh, x_s == x), y_s == y)

        @pl.when(jnp.logical_not(jnp.logical_and(same, same_home)))
        def _():
            greet((zh_s, x_s, y_s, c, line_of(zh_s, by * 3 + bz)))

        return carry

    lax.fori_loop(0, 32, greet_source, 0)

    def greet_tile(n, carry):
        device, same = tile_from(lax.div(n, 3), lax.rem(n, 3))

        @pl.when(jnp.logical_not(same))
        def _():
            greet(device)

        return carry

    lax.fori_loop(0, 12, greet_tile, 0)

    for load in loads:
        load.wait()
    for side, (block, eps, sign) in enumerate(((occ, eps_occ, 1.0), (vir, eps_vir, -1.0))):
        rows_t[...] = block[:, pl.ds(pl.multiple_of(own * 128, 128), 128)].T
        rows = rows_t[pl.ds(pl.multiple_of(y * 16, 16), 16), :]
        for t in range(8):
            high, low = halves(rows * jnp.exp(eps[...] * (sign * tau[t])))
            left[side, t * 16 : t * 16 + 16, :] = high
            left[side, 128 + t * 16 : 144 + t * 16, :] = low

    def partial_sums(d):
        for z in range(2):
            col = lax.rem(own + z * 4 + lax.rem(x + d, 4), 12)
            for side, block in enumerate((occ, vir)):
                high, low = halves(block[:, pl.ds(pl.multiple_of(col * 128, 128), 128)])
                both = dot(left[side], high)
                part[d, z, side * 128 : side * 128 + 128, :] = (
                    both[:128] + both[128:] + dot(left[side, :128, :], low)
                )

    partial_sums(2)
    is_self = same_home.astype(jnp.int32)
    tile_self = jnp.int32(0)
    for h in range(2):
        tile_self = tile_self + (tile_to(zl, h)[2]).astype(jnp.int32)
    inner = (bz > 0).astype(jnp.int32) + (bz < 2).astype(jnp.int32)
    pl.semaphore_wait(barrier, 5 + inner + 32 - is_self + 12 - tile_self)

    right_dev, left_dev = at(x_=x_right), at(x_=x_left)
    sends = [
        remote(part.at[2, 0], half_in.at[0], x_send.at[0], x_recv.at[0], right_dev),
        remote(part.at[2, 1], half_in.at[1], x_send.at[1], x_recv.at[1], left_dev),
        remote(part.at[1, 1], from_side.at[0, 1], x_send.at[2], x_recv.at[2], right_dev),
        remote(part.at[3, 0], from_side.at[1, 0], x_send.at[3], x_recv.at[3], left_dev),
        remote(part.at[1, 0], from_side.at[0, 0], x_send.at[4], x_recv.at[4], right_dev),
        remote(part.at[3, 1], from_side.at[1, 1], x_send.at[5], x_recv.at[5], left_dev),
    ]
    sends[0].start()
    sends[1].start()
    partial_sums(1)
    partial_sums(3)
    sends[2].start()
    sends[3].start()
    partial_sums(0)
    sends[0].wait_recv()
    part[1, 0] = part[1, 0] + half_in[0]
    sends[4].start()
    sends[1].wait_recv()
    part[3, 1] = part[3, 1] + half_in[1]
    sends[5].start()

    load_v.wait()

    def split_v(n, carry):
        rows = pl.ds(pl.multiple_of(n * 64, 64), 64)
        high, low = halves(v_full[rows, :])
        v_high[rows, :] = high
        v_low[rows, :] = low
        return carry

    lax.fori_loop(0, 24, split_v, 0)
    for t in range(8):
        tables[t : t + 1, :] = jnp.cos(omega[...] * tau[t]) * tweight[t]
    for n in range(2, 6):
        sends[n].wait_recv()

    z_out[...] = part[0, other] + from_side[0, other] + from_side[1, other]
    cross = remote(z_out, z_in, z_send, z_recv, at(zh_=other, zl_=5 - zl))
    cross.start()
    z_keep = part[0, zh] + from_side[0, zh] + from_side[1, zh]
    half_in[0] = z_keep
    cross.wait_recv()
    times[...] = -2.0 * (half_in[0, :128, :] + z_in[:128, :]) * (half_in[0, 128:, :] + z_in[128:, :])

    table = tables[...]
    for k in range(32):
        total = table[0:1, k : k + 1] * times[0:16, :]
        for t in range(1, 8):
            total = total + table[t : t + 1, k : k + 1] * times[t * 16 : t * 16 + 16, :]
        freqs[k] = total

    member = zh * 4 + x
    place = blocks.at[own, bx, lax.div(member, 2), pl.ds(pl.multiple_of(y * 16, 16), 16), :]
    mine = (zh * 4 + x_freq) * 4 + slot_freq

    def send_freq(n, carry):
        k = lax.rem(mine + n, 32)
        remote(freqs.at[k], place, a_send, a_recv, freq_to(k)).start()
        return carry

    lax.fori_loop(1, 32, send_freq, 0)

    @pl.when(same_home)
    def _():
        pltpu.make_async_copy(freqs.at[mine], place, a_recv).start()

    @pl.when(jnp.logical_not(same_home))
    def _():
        remote(freqs.at[mine], place, a_self, a_recv, freq_to(mine)).start()

    own_block = blocks.at[home, bx]
    pltpu.make_async_copy(own_block, own_block, a_recv).wait()

    def expand(i, par, m2):
        m = 2 * m2 + par
        col = lax.rem(i + m, 12)
        here = pl.ds(pl.multiple_of(i * 128, 128), 128)
        there = pl.ds(pl.multiple_of(col * 128, 128), 128)
        value = blocks[i, par, m2]
        high, low = halves(value)
        p_high[here, there] = high
        p_low[here, there] = low

        @pl.when(m > 0)
        def _():
            high_t, low_t = halves(value.T)
            p_high[there, here] = high_t
            p_low[there, here] = low_t

    others = (bz, jnp.where(bz == 1, 0, 1), jnp.where(bz == 2, 0, 2))
    pair_devices = {"x": at(x_=x + 1 - 2 * bx), "y": at(y_=y + 1 - 2 * by)}
    middle = bz == 1
    up, down = 1, -1

    def source(piece, core):
        m2, ez, ex, ey = piece
        par = bx if ex == 0 else 1 - bx
        side = by if ey == 0 else 1 - by
        i = (side * 3 + others[ez]) * 2 + core
        live = None if m2 < 3 else jnp.logical_and(par == 0, side == 0)
        return i, par, live

    def guarded(live, action):
        if live is None:
            action()
        else:
            pl.when(live)(action)

    def copy_of(n, piece, lane, device):
        i, par, _live = source(piece, c)
        ref = blocks.at[i, par, piece[0]]
        return remote(ref, ref, g_send.at[lane, n], g_recv.at[n_of(piece)], device)

    def n_of(piece):
        m2, ez, ex, ey = piece
        par = bx if ex == 0 else 1 - bx
        side = by if ey == 0 else 1 - by
        return ((m2 * 2 + side) * 2 + par) * 3 + others[ez]

    def core_copy(piece, core):
        i, par, _live = source(piece, core)
        ref = blocks.at[i, par, piece[0]]
        n = n_of(piece)
        return remote(ref, ref, c_send.at[n], c_recv.at[n], at(c_=1 - c))

    def arrival(piece):
        m2, ez, ex, ey = piece
        moved = {"z": ez, "x": ex, "y": ey}
        return max((p for p, d in enumerate(SPREAD[m2]) if moved[d]), default=-1)

    def sends_of(n, piece):
        m2, ez, _ex, _ey = piece
        last = arrival(piece)
        found = []
        for axis in SPREAD[m2][last + 1 :]:
            if axis == "z":
                found.append((bz < 2, copy_of(n, piece, 0, neighbour(up))))
                found.append((bz > 0, copy_of(n, piece, 1, neighbour(down))))
            else:
                found.append((None, copy_of(n, piece, 2 if axis == "x" else 3, pair_devices[axis])))
        if last >= 0 and SPREAD[m2][last] == "z":
            lane, step = (0, up) if ez == 1 else (1, down)
            found.append((middle, copy_of(n, piece, lane, neighbour(step))))
        return found

    def pick(values, q):
        found = values[-1]
        for at_q in range(len(values) - 2, -1, -1):
            found = jnp.where(q == at_q, values[at_q], found)
        return found

    def unfold(batch, cores):
        def step(q, carry):
            index = pick([t[0] for t in batch], q)
            ex, ey = pick([t[2] for t in batch], q), pick([t[3] for t in batch], q)
            sz = pick([others[t[1]] for t in batch], q)
            theirs = pick(cores, q)
            par, side = bx + ex - 2 * bx * ex, by + ey - 2 * by * ey
            core = c + theirs - 2 * c * theirs
            i = (side * 3 + sz) * 2 + core

            @pl.when(jnp.logical_or(index < 3, jnp.logical_and(par == 0, side == 0)))
            def _():
                @pl.when(theirs == 1)
                def _():
                    ref = blocks.at[i, par, index]
                    n = ((index * 2 + side) * 2 + par) * 3 + sz
                    remote(ref, ref, c_send.at[n], c_recv.at[n], at(c_=1 - c)).wait_recv()

                expand(i, par, index)

            return carry

        lax.fori_loop(0, len(batch), step, 0)

    batches = [PIECES[n : n + BATCH] for n in range(0, len(PIECES), BATCH)]
    for b in range(len(batches) + 1):
        if b < len(batches):
            for q, piece in enumerate(batches[b]):
                _i, _par, live = source(piece, c)

                def take(n=b * BATCH + q, piece=piece):
                    if arrival(piece) >= 0:
                        copy_of(n, piece, 0, neighbour(up)).wait_recv()
                    for when, copy in sends_of(n, piece):
                        guarded(when, copy.start)
                    core_copy(piece, c).start()

                guarded(live, take)
        mine_now = batches[b] if b < len(batches) else ()
        theirs_now = batches[b - 1] if b else ()
        unfold(mine_now + theirs_now, [0] * len(mine_now) + [1] * len(theirs_now))

    rows = pl.ds(pl.multiple_of(strip * 64, 64), 64)
    stack_a[:64, :] = v_high[rows, :]
    stack_a[64:, :] = v_low[rows, :]

    def product(src, high, low, use):
        def step(n, carry):
            cols = pl.ds(pl.multiple_of(n * 256, 256), 256)
            both = dot(src[...], high[:, cols])
            use(n, cols, both[:64] + both[64:] + dot(src[:64, :], low[:, cols]))
            return carry

        lax.fori_loop(0, 6, step, 0)

    def keep(dst, cols, value):
        high, low = halves(value)
        dst[:64, cols] = high
        dst[64:, cols] = low

    def use_one(n, cols, value):
        first[:, cols] = value
        keep(stack_b, cols, value)

    def send_tile(n, cols, value):
        tiles[n] = value
        for h in range(2):
            q, slot, same = tile_to(n, h)
            src = tiles.at[n, pl.ds(32 * h, 32), :]
            dst = landed.at[slot_freq, slot]

            @pl.when(same)
            def _():
                pltpu.make_async_copy(src, dst, o_recv).start()

            @pl.when(jnp.logical_not(same))
            def _():
                remote(src, dst, o_send.at[2 * n + h], o_recv, at(x_=x_freq, y_=lax.div(q, 2), c_=lax.rem(q, 2), zl_=n)).start()

    product(stack_a, p_high, p_low, use_one)
    product(stack_b, v_high, v_low, lambda n, cols, value: keep(stack_a, cols, value))
    product(stack_a, p_high, p_low, lambda n, cols, value: keep(stack_b, cols, first[:, cols] + value))
    product(stack_b, v_high, v_low, send_tile)

    for n in range(6):
        sends[n].wait_send()
    cross.wait_send()
    pltpu.make_async_copy(freqs.at[pl.ds(0, 31)], freqs.at[pl.ds(0, 31)], a_send).wait()

    @pl.when(jnp.logical_not(same_home))
    def _():
        pltpu.make_async_copy(freqs.at[0], freqs.at[0], a_self).wait()

    for n, piece in enumerate(PIECES):
        _i, _par, live = source(piece, c)

        def drain(n=n, piece=piece):
            for when, copy in sends_of(n, piece):
                guarded(when, copy.wait_send)
            core_copy(piece, c).wait_send()

        guarded(live, drain)

    pltpu.make_async_copy(landed, landed, o_recv).wait()
    out[...] = landed[...].reshape(out.shape)

    def drain_tiles(n, carry):
        col, h = lax.div(n, 2), lax.rem(n, 2)
        same = tile_to(col, h)[2]

        @pl.when(jnp.logical_not(same))
        def _():
            src = tiles.at[0, pl.ds(0, 32), :]
            pltpu.make_async_copy(src, src, o_send.at[n]).wait()

        return carry

    lax.fori_loop(0, 12, drain_tiles, 0)


def on_device(c_occ, c_vir, eps_occ, eps_vir, tau, tweight, omega, coulomb):
    grid = coulomb.shape[0]
    width = c_occ.shape[1]
    dma = pltpu.SemaphoreType.DMA
    hbm = pl.BlockSpec(memory_space=pl.ANY)
    vmem, smem = pl.BlockSpec(memory_space=pltpu.VMEM), pl.BlockSpec(memory_space=pltpu.SMEM)
    return pl.pallas_call(
        kernel,
        out_shape=jax.ShapeDtypeStruct((4, 96, 256), F32),
        in_specs=[smem, smem, vmem, vmem, vmem, hbm, hbm, hbm],
        out_specs=vmem,
        scratch_shapes=[
            pltpu.VMEM((128, width), F32),
            pltpu.VMEM((2, 256, width), BF16),
            pltpu.VMEM((4, 2, 256, 128), F32),
            pltpu.VMEM((2, 256, 128), F32),
            pltpu.VMEM((2, 2, 256, 128), F32),
            pltpu.VMEM((256, 128), F32),
            pltpu.VMEM((256, 128), F32),
            pltpu.VMEM((128, 128), F32),
            pltpu.VMEM((32, 16, 128), F32),
            pltpu.VMEM((12, 2, 4, 128, 128), F32),
            pltpu.VMEM((grid, grid), BF16),
            pltpu.VMEM((grid, grid), BF16),
            pltpu.VMEM((grid, grid), F32),
            pltpu.VMEM((grid, grid), BF16),
            pltpu.VMEM((grid, grid), BF16),
            pltpu.VMEM((64, grid), F32),
            pltpu.VMEM((128, grid), BF16),
            pltpu.VMEM((128, grid), BF16),
            pltpu.VMEM((6, 64, 256), F32),
            pltpu.VMEM((4, 3, 32, 256), F32),
            pltpu.VMEM((8, omega.shape[0]), F32),
            pltpu.VMEM((width, grid), F32),
            pltpu.VMEM((width, grid), F32),
            dma((2,)), dma, dma((6,)), dma((6,)), dma, dma, dma, dma, dma,
            dma((4, 48)), dma((48,)), dma((48,)), dma((48,)), dma((12,)), dma,
        ],
        compiler_params=pltpu.CompilerParams(
            collective_id=0, has_side_effects=True, vmem_limit_bytes=60 * 1024 * 1024
        ),
        name="screened",
    )(tau, tweight, omega[None, :], eps_occ[None, :], eps_vir[None, :], c_occ.T, c_vir.T, coulomb)


def solution(mesh):
    split = Mesh(mesh.devices.reshape(2, 4, 8, 2, 6), AXES)
    tm = ("zh", "x")
    placed = (P(None, tm), P(None, tm), P(tm), P(tm), P(), P(), P(), P())
    return jax.shard_map(
        on_device, mesh=split, in_specs=placed, out_specs=P(tm, ("y", "c"), "zl"), check_vma=False
    )
```

```python
import jax
import jax.numpy as jnp
from jax import lax
from jax.experimental import pallas as pl
from jax.experimental.pallas import tpu as pltpu
from jax.sharding import Mesh
from jax.sharding import PartitionSpec as P

AXES = ("zh", "x", "y", "c", "zl")
MESH_ID = pl.DeviceIdType.MESH
F32, BF16 = jnp.float32, jnp.bfloat16

BATCH = 4
SPREAD = ("xzy", "yzx", "zxy", "yzx")
PIECES = (
    (0, 0, 0, 0), (1, 0, 0, 0), (0, 0, 1, 0), (0, 1, 0, 0), (0, 0, 0, 1), (2, 0, 0, 0),
    (3, 0, 0, 0), (1, 0, 0, 1), (1, 1, 0, 0), (1, 0, 1, 0), (0, 2, 0, 0), (0, 1, 1, 0),
    (0, 1, 0, 1), (0, 0, 1, 1), (2, 0, 1, 0), (2, 1, 0, 0), (3, 0, 1, 0), (1, 2, 0, 0),
    (2, 0, 0, 1), (1, 1, 1, 0), (1, 0, 1, 1), (3, 1, 0, 0), (0, 2, 1, 0), (1, 1, 0, 1),
    (3, 0, 0, 1), (0, 2, 0, 1), (2, 1, 1, 0), (2, 2, 0, 0), (0, 1, 1, 1), (3, 2, 0, 0),
    (2, 0, 1, 1), (1, 2, 1, 0), (3, 1, 1, 0), (1, 2, 0, 1), (3, 0, 1, 1), (1, 1, 1, 1),
    (3, 1, 0, 1), (2, 1, 0, 1), (2, 2, 1, 0), (0, 2, 1, 1), (3, 2, 0, 1), (3, 2, 1, 0),
    (2, 1, 1, 1), (2, 2, 0, 1), (1, 2, 1, 1), (3, 1, 1, 1), (3, 2, 1, 1), (2, 2, 1, 1),
)


def halves(value):
    high = value.astype(BF16)
    return high, (value - high.astype(F32)).astype(BF16)


def dot(a, b):
    return lax.dot_general(a, b, (((1,), (0,)), ((), ())), preferred_element_type=F32)


def remote(src, dst, send, recv, device):
    return pltpu.make_async_remote_copy(
        src_ref=src, dst_ref=dst, send_sem=send, recv_sem=recv, device_id=device, device_id_type=MESH_ID
    )


def kernel(
    tau, tweight, omega, eps_occ, eps_vir, occ_in, vir_in, coulomb, out,
    rows_t, left, part, half_in, from_side, z_out, z_in, z_keep, times, freqs, blocks,
    p_high, p_low, v_full, v_high, v_low, first, stack_a, stack_b, tiles, landed,
    tables, occ, vir, b_sem, v_sem, x_send, x_recv, z_send, z_recv, a_send, a_self, a_recv,
    g_send, g_recv, c_send, c_recv, o_send, o_recv,
):
    zh, x, y, c, zl = (lax.axis_index(a) for a in AXES)
    level = zl + zh * (5 - 2 * zl)
    own = level * 2 + c
    triple, bz = lax.div(level, 3), lax.rem(level, 3)
    x_pair, bx = lax.div(x, 2), lax.rem(x, 2)
    y_pair, by = lax.div(y, 2), lax.rem(y, 2)
    x_freq = 2 * x_pair + lax.rem(y_pair, 2)
    slot_freq = 2 * lax.div(y_pair, 2) + triple
    home = (by * 3 + bz) * 2 + c
    x_right, x_left = lax.rem(x + 1, 4), lax.rem(x + 3, 4)
    other = 1 - zh

    def at(zh_=zh, x_=x, y_=y, c_=c, zl_=zl):
        return (zh_, x_, y_, c_, zl_)

    def line_of(zh_, level_):
        return level_ + zh_ * (5 - 2 * level_)

    load_v = pltpu.make_async_copy(coulomb, v_full, v_sem)
    loads = [
        pltpu.make_async_copy(occ_in, occ, b_sem.at[0]),
        pltpu.make_async_copy(vir_in, vir, b_sem.at[1]),
    ]
    for load in loads:
        load.start()
    load_v.start()

    barrier = pltpu.get_barrier_semaphore()

    def greet(device):
        pl.semaphore_signal(barrier, inc=1, device_id=device, device_id_type=MESH_ID)

    strip = lax.rem(6 * (2 * by + bx) + c * 3 + bz + 6 * y_pair + 15, 24)

    def tile_to(col, h):
        half = 2 * strip + h
        q = lax.div(half, 3)
        same = jnp.logical_and(jnp.logical_and(q == 2 * y + c, col == zl), x_freq == x)
        return q, lax.rem(half, 3), same

    def tile_from(f, slot):
        y_pair_s = 2 * lax.div(f, 2) + bx
        r = lax.div(3 * (2 * y + c) + slot, 2)
        u = lax.rem(r + 81 - 6 * y_pair_s, 24)
        a, b = lax.div(u, 6), lax.rem(u, 6)
        x_s, y_s = 2 * x_pair + lax.rem(a, 2), 2 * y_pair_s + lax.div(a, 2)
        zl_s, c_s = line_of(zh, 3 * lax.rem(f, 2) + lax.rem(b, 3)), lax.div(b, 3)
        same = jnp.logical_and(
            jnp.logical_and(y_s == y, c_s == c), jnp.logical_and(zl_s == zl, x_s == x)
        )
        return at(x_=x_s, y_=y_s, c_=c_s, zl_=zl_s), same

    def freq_to(k):
        zh_k, x_k, f = lax.div(k, 16), lax.rem(lax.div(k, 4), 4), lax.rem(k, 4)
        x_d = 2 * lax.div(x_k, 2) + bx
        y_d = 2 * (2 * lax.div(f, 2) + lax.rem(x_k, 2)) + triple
        return (zh_k, x_d, y_d, c, line_of(zh_k, 3 * lax.rem(f, 2) + bz))

    greet(at(x_=x_left))
    greet(at(x_=x_right))
    greet(at(zh_=other, zl_=5 - zl))
    greet(at(y_=y + 1 - 2 * by))
    greet(at(c_=1 - c))

    def neighbour(step):
        return at(zl_=line_of(zh, level + step))

    @pl.when(bz > 0)
    def _():
        greet(neighbour(-1))

    @pl.when(bz < 2)
    def _():
        greet(neighbour(1))

    same_home = triple == by

    def greet_source(n, carry):
        zh_s, x_s, y_s = lax.div(n, 16), 2 * lax.rem(lax.div(n, 8), 2) + bx, lax.rem(n, 8)
        same = jnp.logical_and(jnp.logical_and(zh_s == zh, x_s == x), y_s == y)

        @pl.when(jnp.logical_not(jnp.logical_and(same, same_home)))
        def _():
            greet((zh_s, x_s, y_s, c, line_of(zh_s, by * 3 + bz)))

        return carry

    lax.fori_loop(0, 32, greet_source, 0)

    def greet_tile(n, carry):
        device, same = tile_from(lax.div(n, 3), lax.rem(n, 3))

        @pl.when(jnp.logical_not(same))
        def _():
            greet(device)

        return carry

    lax.fori_loop(0, 12, greet_tile, 0)

    for load in loads:
        load.wait()
    for side, (block, eps, sign) in enumerate(((occ, eps_occ, 1.0), (vir, eps_vir, -1.0))):
        rows_t[...] = block[:, pl.ds(pl.multiple_of(own * 128, 128), 128)].T
        rows = rows_t[pl.ds(pl.multiple_of(y * 16, 16), 16), :]
        for t in range(8):
            high, low = halves(rows * jnp.exp(eps[...] * (sign * tau[t])))
            for h in range(2):
                at_row = h * 64 + t * 8
                left[side, at_row : at_row + 8, :] = high[h * 8 : h * 8 + 8]
                left[side, 128 + at_row : 136 + at_row, :] = low[h * 8 : h * 8 + 8]

    def partial_sums(d):
        for z in range(2):
            col = lax.rem(own + z * 4 + lax.rem(x + d, 4), 12)
            for side, block in enumerate((occ, vir)):
                high, low = halves(block[:, pl.ds(pl.multiple_of(col * 128, 128), 128)])
                both = dot(left[side], high)
                whole = both[:128] + both[128:] + dot(left[side, :128, :], low)
                for h in range(2):
                    part[d, z, h, side * 64 : side * 64 + 64, :] = whole[h * 64 : h * 64 + 64]

    partial_sums(2)
    is_self = same_home.astype(jnp.int32)
    tile_self = jnp.int32(0)
    for h in range(2):
        tile_self = tile_self + (tile_to(zl, h)[2]).astype(jnp.int32)
    inner = (bz > 0).astype(jnp.int32) + (bz < 2).astype(jnp.int32)
    pl.semaphore_wait(barrier, 5 + inner + 32 - is_self + 12 - tile_self)

    right_dev, left_dev = at(x_=x_right), at(x_=x_left)

    def ring(n, src, dst, device):
        return [
            remote(src.at[h], dst.at[h], x_send.at[n, h], x_recv.at[n, h], device) for h in range(2)
        ]

    sends = [
        ring(0, part.at[2, 0], half_in.at[0], right_dev),
        ring(1, part.at[2, 1], half_in.at[1], left_dev),
        ring(2, part.at[1, 1], from_side.at[0, 1], right_dev),
        ring(3, part.at[3, 0], from_side.at[1, 0], left_dev),
        ring(4, part.at[1, 0], from_side.at[0, 0], right_dev),
        ring(5, part.at[3, 1], from_side.at[1, 1], left_dev),
    ]
    for h in range(2):
        sends[0][h].start()
        sends[1][h].start()
    partial_sums(1)
    partial_sums(3)
    for h in range(2):
        sends[2][h].start()
        sends[3][h].start()
        sends[0][h].wait_recv()
        part[1, 0, h] = part[1, 0, h] + half_in[0, h]
        sends[4][h].start()
        sends[1][h].wait_recv()
        part[3, 1, h] = part[3, 1, h] + half_in[1, h]
        sends[5][h].start()
        if h == 0:
            partial_sums(0)
    for t in range(8):
        tables[t : t + 1, :] = jnp.cos(omega[...] * tau[t]) * tweight[t]

    load_v.wait()

    def split_v(n, carry):
        rows = pl.ds(pl.multiple_of(n * 64, 64), 64)
        high, low = halves(v_full[rows, :])
        v_high[rows, :] = high
        v_low[rows, :] = low
        return carry

    lax.fori_loop(0, 24, split_v, 0)

    cross = [
        remote(z_out.at[h], z_in.at[h], z_send.at[h], z_recv.at[h], at(zh_=other, zl_=5 - zl))
        for h in range(2)
    ]
    for h in range(2):
        for n in range(2, 6):
            sends[n][h].wait_recv()
        z_out[h] = part[0, other, h] + from_side[0, other, h] + from_side[1, other, h]
        cross[h].start()
        z_keep[h] = part[0, zh, h] + from_side[0, zh, h] + from_side[1, zh, h]

    member = zh * 4 + x
    mine = (zh * 4 + x_freq) * 4 + slot_freq
    table = tables[...]
    for h in range(2):
        cross[h].wait_recv()
        for t in range(8):
            green = [z_keep[h, v * 64 + t * 8 : v * 64 + t * 8 + 8, :] for v in range(2)]
            rest = [z_in[h, v * 64 + t * 8 : v * 64 + t * 8 + 8, :] for v in range(2)]
            times[t] = -2.0 * (green[0] + rest[0]) * (green[1] + rest[1])
        for k in range(32):
            total = table[0:1, k : k + 1] * times[0]
            for t in range(1, 8):
                total = total + table[t : t + 1, k : k + 1] * times[t]
            freqs[h, k] = total
        place = blocks.at[own, bx, lax.div(member, 2), pl.ds(pl.multiple_of(y * 16 + h * 8, 8), 8), :]

        def send_freq(n, carry, h=h, place=place):
            k = lax.rem(mine + n, 32)
            remote(freqs.at[h, k], place, a_send.at[h], a_recv.at[lax.div(member, 2)], freq_to(k)).start()
            return carry

        lax.fori_loop(1, 32, send_freq, 0)

        @pl.when(same_home)
        def _(h=h, place=place):
            pltpu.make_async_copy(freqs.at[h, mine], place, a_recv.at[lax.div(member, 2)]).start()

        @pl.when(jnp.logical_not(same_home))
        def _(h=h, place=place):
            remote(freqs.at[h, mine], place, a_self.at[h], a_recv.at[lax.div(member, 2)], freq_to(mine)).start()

    def expand(i, par, m2):
        m = 2 * m2 + par
        col = lax.rem(i + m, 12)
        here = pl.ds(pl.multiple_of(i * 128, 128), 128)
        there = pl.ds(pl.multiple_of(col * 128, 128), 128)
        value = blocks[i, par, m2]
        high, low = halves(value)
        p_high[here, there] = high
        p_low[here, there] = low

        @pl.when(m > 0)
        def _():
            high_t, low_t = halves(value.T)
            p_high[there, here] = high_t
            p_low[there, here] = low_t

    others = (bz, jnp.where(bz == 1, 0, 1), jnp.where(bz == 2, 0, 2))
    pair_devices = {"x": at(x_=x + 1 - 2 * bx), "y": at(y_=y + 1 - 2 * by)}
    middle = bz == 1
    up, down = 1, -1

    def quarter(q):
        return lax.rem(q + 2 * zh, 4)

    def source(piece, core):
        m2, ez, ex, ey = piece
        par = bx if ex == 0 else 1 - bx
        side = by if ey == 0 else 1 - by
        i = (side * 3 + others[ez]) * 2 + core
        small = jnp.logical_and(par == 0, side == 0)
        live = None if m2 % 2 == 0 else jnp.logical_or(quarter(m2) < 3, small)
        return i, par, live

    def guarded(live, action):
        if live is None:
            action()
        else:
            pl.when(live)(action)

    def copy_of(n, piece, lane, device):
        i, par, _live = source(piece, c)
        ref = blocks.at[i, par, quarter(piece[0])]
        return remote(ref, ref, g_send.at[lane, n], g_recv.at[n_of(piece)], device)

    def n_of(piece):
        m2, ez, ex, ey = piece
        par = bx if ex == 0 else 1 - bx
        side = by if ey == 0 else 1 - by
        return ((quarter(m2) * 2 + side) * 2 + par) * 3 + others[ez]

    def core_copy(piece, core):
        i, par, _live = source(piece, core)
        ref = blocks.at[i, par, quarter(piece[0])]
        n = n_of(piece)
        return remote(ref, ref, c_send.at[n], c_recv.at[n], at(c_=1 - c))

    def arrival(piece):
        m2, ez, ex, ey = piece
        moved = {"z": ez, "x": ex, "y": ey}
        return max((p for p, d in enumerate(SPREAD[m2]) if moved[d]), default=-1)

    def sends_of(n, piece):
        m2, ez, _ex, _ey = piece
        last = arrival(piece)
        found = []
        for axis in SPREAD[m2][last + 1 :]:
            if axis == "z":
                found.append((bz < 2, copy_of(n, piece, 0, neighbour(up))))
                found.append((bz > 0, copy_of(n, piece, 1, neighbour(down))))
            else:
                found.append((None, copy_of(n, piece, 2 if axis == "x" else 3, pair_devices[axis])))
        if last >= 0 and SPREAD[m2][last] == "z":
            lane, step = (0, up) if ez == 1 else (1, down)
            found.append((middle, copy_of(n, piece, lane, neighbour(step))))
        return found

    def pick(values, q):
        found = values[-1]
        for at_q in range(len(values) - 2, -1, -1):
            found = jnp.where(q == at_q, values[at_q], found)
        return found

    def unfold(batch, cores):
        def step(q, carry):
            index = quarter(pick([t[0] for t in batch], q))
            ex, ey = pick([t[2] for t in batch], q), pick([t[3] for t in batch], q)
            sz = pick([others[t[1]] for t in batch], q)
            theirs = pick(cores, q)
            par, side = bx + ex - 2 * bx * ex, by + ey - 2 * by * ey
            core = c + theirs - 2 * c * theirs
            i = (side * 3 + sz) * 2 + core

            @pl.when(jnp.logical_or(index < 3, jnp.logical_and(par == 0, side == 0)))
            def _():
                @pl.when(theirs == 1)
                def _():
                    ref = blocks.at[i, par, index]
                    n = ((index * 2 + side) * 2 + par) * 3 + sz
                    remote(ref, ref, c_send.at[n], c_recv.at[n], at(c_=1 - c)).wait_recv()

                expand(i, par, index)

            return carry

        lax.fori_loop(0, len(batch), step, 0)

    batches = [PIECES[n : n + BATCH] for n in range(0, len(PIECES), BATCH)]
    for b in range(len(batches) + 1):
        if b < len(batches):
            for q, piece in enumerate(batches[b]):
                _i, _par, live = source(piece, c)

                def take(n=b * BATCH + q, piece=piece):
                    if arrival(piece) >= 0:
                        copy_of(n, piece, 0, neighbour(up)).wait_recv()
                    for when, copy in sends_of(n, piece):
                        guarded(when, copy.start)
                    core_copy(piece, c).start()

                if arrival(piece) < 0:
                    ref = blocks.at[home, bx, quarter(piece[0])]
                    pltpu.make_async_copy(ref, ref, a_recv.at[quarter(piece[0])]).wait()
                guarded(live, take)
        mine_now = batches[b] if b < len(batches) else ()
        theirs_now = batches[b - 1] if b else ()
        unfold(mine_now + theirs_now, [0] * len(mine_now) + [1] * len(theirs_now))

    rows = pl.ds(pl.multiple_of(strip * 64, 64), 64)
    stack_a[:64, :] = v_high[rows, :]
    stack_a[64:, :] = v_low[rows, :]

    def product(src, high, low, use, start=0):
        def step(n, carry):
            n = lax.rem(n + start, 6)
            cols = pl.ds(pl.multiple_of(n * 256, 256), 256)
            both = dot(src[...], high[:, cols])
            use(n, cols, both[:64] + both[64:] + dot(src[:64, :], low[:, cols]))
            return carry

        lax.fori_loop(0, 6, step, 0)

    def keep(dst, cols, value):
        high, low = halves(value)
        dst[:64, cols] = high
        dst[64:, cols] = low

    def use_one(n, cols, value):
        first[:, cols] = value
        keep(stack_b, cols, value)

    def send_tile(n, cols, value):
        tiles[n] = value
        for h in range(2):
            q, slot, same = tile_to(n, h)
            src = tiles.at[n, pl.ds(32 * h, 32), :]
            dst = landed.at[slot_freq, slot]

            @pl.when(same)
            def _():
                pltpu.make_async_copy(src, dst, o_recv).start()

            @pl.when(jnp.logical_not(same))
            def _():
                remote(src, dst, o_send.at[2 * n + h], o_recv, at(x_=x_freq, y_=lax.div(q, 2), c_=lax.rem(q, 2), zl_=n)).start()

    product(stack_a, p_high, p_low, use_one)
    product(stack_b, v_high, v_low, lambda n, cols, value: keep(stack_a, cols, value))
    product(stack_a, p_high, p_low, lambda n, cols, value: keep(stack_b, cols, first[:, cols] + value))
    product(stack_b, v_high, v_low, send_tile, jnp.where(zl < 3, 3, 0))

    for h in range(2):
        for n in range(6):
            sends[n][h].wait_send()
        cross[h].wait_send()
        sent = freqs.at[h, pl.ds(0, 31)]
        pltpu.make_async_copy(sent, sent, a_send.at[h]).wait()

        @pl.when(jnp.logical_not(same_home))
        def _(h=h):
            pltpu.make_async_copy(freqs.at[h, 0], freqs.at[h, 0], a_self.at[h]).wait()

    for n, piece in enumerate(PIECES):
        _i, _par, live = source(piece, c)

        def drain(n=n, piece=piece):
            for when, copy in sends_of(n, piece):
                guarded(when, copy.wait_send)
            core_copy(piece, c).wait_send()

        guarded(live, drain)

    pltpu.make_async_copy(landed, landed, o_recv).wait()
    out[...] = landed[...].reshape(out.shape)

    def drain_tiles(n, carry):
        col, h = lax.div(n, 2), lax.rem(n, 2)
        same = tile_to(col, h)[2]

        @pl.when(jnp.logical_not(same))
        def _():
            src = tiles.at[0, pl.ds(0, 32), :]
            pltpu.make_async_copy(src, src, o_send.at[n]).wait()

        return carry

    lax.fori_loop(0, 12, drain_tiles, 0)


def on_device(c_occ, c_vir, eps_occ, eps_vir, tau, tweight, omega, coulomb):
    grid = coulomb.shape[0]
    width = c_occ.shape[1]
    dma = pltpu.SemaphoreType.DMA
    hbm = pl.BlockSpec(memory_space=pl.ANY)
    vmem, smem = pl.BlockSpec(memory_space=pltpu.VMEM), pl.BlockSpec(memory_space=pltpu.SMEM)
    return pl.pallas_call(
        kernel,
        out_shape=jax.ShapeDtypeStruct((4, 96, 256), F32),
        in_specs=[smem, smem, vmem, vmem, vmem, hbm, hbm, hbm],
        out_specs=vmem,
        scratch_shapes=[
            pltpu.VMEM((128, width), F32),
            pltpu.VMEM((2, 256, width), BF16),
            pltpu.VMEM((4, 2, 2, 128, 128), F32),
            pltpu.VMEM((2, 2, 128, 128), F32),
            pltpu.VMEM((2, 2, 2, 128, 128), F32),
            pltpu.VMEM((2, 128, 128), F32),
            pltpu.VMEM((2, 128, 128), F32),
            pltpu.VMEM((2, 128, 128), F32),
            pltpu.VMEM((8, 8, 128), F32),
            pltpu.VMEM((2, 32, 8, 128), F32),
            pltpu.VMEM((12, 2, 4, 128, 128), F32),
            pltpu.VMEM((grid, grid), BF16),
            pltpu.VMEM((grid, grid), BF16),
            pltpu.VMEM((grid, grid), F32),
            pltpu.VMEM((grid, grid), BF16),
            pltpu.VMEM((grid, grid), BF16),
            pltpu.VMEM((64, grid), F32),
            pltpu.VMEM((128, grid), BF16),
            pltpu.VMEM((128, grid), BF16),
            pltpu.VMEM((6, 64, 256), F32),
            pltpu.VMEM((4, 3, 32, 256), F32),
            pltpu.VMEM((8, omega.shape[0]), F32),
            pltpu.VMEM((width, grid), F32),
            pltpu.VMEM((width, grid), F32),
            dma((2,)), dma, dma((6, 2)), dma((6, 2)), dma((2,)), dma((2,)), dma((2,)), dma((2,)), dma((4,)),
            dma((4, 48)), dma((48,)), dma((48,)), dma((48,)), dma((12,)), dma,
        ],
        compiler_params=pltpu.CompilerParams(
            collective_id=0, has_side_effects=True, vmem_limit_bytes=60 * 1024 * 1024
        ),
        name="screened",
    )(tau, tweight, omega[None, :], eps_occ[None, :], eps_vir[None, :], c_occ.T, c_vir.T, coulomb)


def solution(mesh):
    split = Mesh(mesh.devices.reshape(2, 4, 8, 2, 6), AXES)
    tm = ("zh", "x")
    placed = (P(None, tm), P(None, tm), P(tm), P(tm), P(), P(), P(), P())
    return jax.shard_map(
        on_device, mesh=split, in_specs=placed, out_specs=P(tm, ("y", "c"), "zl"), check_vma=False
    )
```

```python
import jax
import jax.numpy as jnp
from jax import lax
from jax.experimental import pallas as pl
from jax.experimental.pallas import tpu as pltpu
from jax.sharding import Mesh
from jax.sharding import PartitionSpec as P

AXES = ("zh", "x", "y", "c", "zl")
MESH_ID = pl.DeviceIdType.MESH
F32, BF16 = jnp.float32, jnp.bfloat16

BATCH = 4
SPREAD = ("xzy", "yzx", "zxy", "yzx")
PIECES = (
    (0, 0, 0, 0), (1, 0, 0, 0), (0, 0, 1, 0), (2, 0, 0, 0), (1, 1, 0, 0), (3, 0, 0, 0),
    (0, 1, 0, 0), (1, 0, 0, 1), (2, 0, 1, 0), (2, 1, 0, 0), (0, 0, 1, 1), (1, 2, 0, 0),
    (3, 0, 0, 1), (1, 1, 1, 0), (3, 1, 0, 0), (0, 1, 1, 0), (0, 2, 0, 0), (0, 1, 0, 1),
    (1, 1, 0, 1), (0, 0, 0, 1), (2, 0, 0, 1), (2, 2, 0, 0), (2, 0, 1, 1), (1, 0, 1, 0),
    (3, 2, 0, 0), (2, 1, 1, 0), (3, 0, 1, 0), (1, 0, 1, 1), (0, 2, 1, 0), (3, 1, 0, 1),
    (1, 2, 1, 0), (1, 2, 0, 1), (0, 2, 0, 1), (2, 2, 1, 0), (0, 1, 1, 1), (3, 2, 0, 1),
    (3, 1, 1, 1), (3, 1, 1, 0), (2, 1, 1, 1), (2, 2, 0, 1), (3, 2, 1, 0), (1, 2, 1, 1),
    (2, 1, 0, 1), (0, 2, 1, 1), (2, 2, 1, 1), (3, 0, 1, 1), (1, 1, 1, 1), (3, 2, 1, 1),
)


def halves(value):
    high = value.astype(BF16)
    return high, (value - high.astype(F32)).astype(BF16)


def dot(a, b):
    return lax.dot_general(a, b, (((1,), (0,)), ((), ())), preferred_element_type=F32)


def remote(src, dst, send, recv, device):
    return pltpu.make_async_remote_copy(
        src_ref=src, dst_ref=dst, send_sem=send, recv_sem=recv, device_id=device, device_id_type=MESH_ID
    )


def kernel(
    tau, tweight, omega, eps_occ, eps_vir, occ_in, vir_in, coulomb, out,
    rows_t, left, part, half_in, from_side, z_out, z_in, z_keep, times, freqs, blocks,
    p_high, p_low, v_full, v_high, v_low, first, stack_a, stack_b, tiles, landed,
    tables, occ, vir, b_sem, v_sem, x_send, x_recv, z_send, z_recv, a_send, a_self, a_recv,
    g_send, g_recv, c_send, c_recv, o_send, o_recv,
):
    zh, x, y, c, zl = (lax.axis_index(a) for a in AXES)
    level = zl + zh * (5 - 2 * zl)
    own = level * 2 + c
    triple, bz = lax.div(level, 3), lax.rem(level, 3)
    x_pair, bx = lax.div(x, 2), lax.rem(x, 2)
    y_pair, by = lax.div(y, 2), lax.rem(y, 2)
    x_freq = 2 * x_pair + lax.rem(y_pair, 2)
    slot_freq = 2 * lax.div(y_pair, 2) + triple
    home = (by * 3 + bz) * 2 + c
    x_right, x_left = lax.rem(x + 1, 4), lax.rem(x + 3, 4)
    other = 1 - zh

    def at(zh_=zh, x_=x, y_=y, c_=c, zl_=zl):
        return (zh_, x_, y_, c_, zl_)

    def line_of(zh_, level_):
        return level_ + zh_ * (5 - 2 * level_)

    load_v = pltpu.make_async_copy(coulomb, v_full, v_sem)
    loads = [
        pltpu.make_async_copy(occ_in, occ, b_sem.at[0]),
        pltpu.make_async_copy(vir_in, vir, b_sem.at[1]),
    ]
    for load in loads:
        load.start()
    load_v.start()

    barrier = pltpu.get_barrier_semaphore()

    def greet(device):
        pl.semaphore_signal(barrier, inc=1, device_id=device, device_id_type=MESH_ID)

    strip = lax.rem(6 * (2 * by + bx) + c * 3 + bz + 6 * y_pair + 15, 24)

    def tile_to(col, h):
        half = 2 * strip + h
        q = lax.div(half, 3)
        same = jnp.logical_and(jnp.logical_and(q == 2 * y + c, col == zl), x_freq == x)
        return q, lax.rem(half, 3), same

    def tile_from(f, slot):
        y_pair_s = 2 * lax.div(f, 2) + bx
        r = lax.div(3 * (2 * y + c) + slot, 2)
        u = lax.rem(r + 81 - 6 * y_pair_s, 24)
        a, b = lax.div(u, 6), lax.rem(u, 6)
        x_s, y_s = 2 * x_pair + lax.rem(a, 2), 2 * y_pair_s + lax.div(a, 2)
        zl_s, c_s = line_of(zh, 3 * lax.rem(f, 2) + lax.rem(b, 3)), lax.div(b, 3)
        same = jnp.logical_and(
            jnp.logical_and(y_s == y, c_s == c), jnp.logical_and(zl_s == zl, x_s == x)
        )
        return at(x_=x_s, y_=y_s, c_=c_s, zl_=zl_s), same

    def freq_to(k):
        zh_k, x_k, f = lax.div(k, 16), lax.rem(lax.div(k, 4), 4), lax.rem(k, 4)
        x_d = 2 * lax.div(x_k, 2) + bx
        y_d = 2 * (2 * lax.div(f, 2) + lax.rem(x_k, 2)) + triple
        return (zh_k, x_d, y_d, c, line_of(zh_k, 3 * lax.rem(f, 2) + bz))

    greet(at(x_=x_left))
    greet(at(x_=x_right))
    greet(at(zh_=other, zl_=5 - zl))
    greet(at(y_=y + 1 - 2 * by))
    greet(at(c_=1 - c))

    def neighbour(step):
        return at(zl_=line_of(zh, level + step))

    @pl.when(bz > 0)
    def _():
        greet(neighbour(-1))

    @pl.when(bz < 2)
    def _():
        greet(neighbour(1))

    same_home = triple == by

    def greet_source(n, carry):
        zh_s, x_s, y_s = lax.div(n, 16), 2 * lax.rem(lax.div(n, 8), 2) + bx, lax.rem(n, 8)
        same = jnp.logical_and(jnp.logical_and(zh_s == zh, x_s == x), y_s == y)

        @pl.when(jnp.logical_not(jnp.logical_and(same, same_home)))
        def _():
            greet((zh_s, x_s, y_s, c, line_of(zh_s, by * 3 + bz)))

        return carry

    lax.fori_loop(0, 32, greet_source, 0)

    def greet_tile(n, carry):
        device, same = tile_from(lax.div(n, 3), lax.rem(n, 3))

        @pl.when(jnp.logical_not(same))
        def _():
            greet(device)

        return carry

    lax.fori_loop(0, 12, greet_tile, 0)

    for load in loads:
        load.wait()
    for side, (block, eps, sign) in enumerate(((occ, eps_occ, 1.0), (vir, eps_vir, -1.0))):
        rows_t[...] = block[:, pl.ds(pl.multiple_of(own * 128, 128), 128)].T
        rows = rows_t[pl.ds(pl.multiple_of(y * 16, 16), 16), :]
        for t in range(8):
            high, low = halves(rows * jnp.exp(eps[...] * (sign * tau[t])))
            for h in range(2):
                at_row = h * 64 + t * 8
                left[side, at_row : at_row + 8, :] = high[h * 8 : h * 8 + 8]
                left[side, 128 + at_row : 136 + at_row, :] = low[h * 8 : h * 8 + 8]

    def partial_sums(d):
        for z in range(2):
            col = lax.rem(own + z * 4 + lax.rem(x + d, 4), 12)
            for side, block in enumerate((occ, vir)):
                high, low = halves(block[:, pl.ds(pl.multiple_of(col * 128, 128), 128)])
                both = dot(left[side], high)
                whole = both[:128] + both[128:] + dot(left[side, :128, :], low)
                for h in range(2):
                    part[d, z, h, side * 64 : side * 64 + 64, :] = whole[h * 64 : h * 64 + 64]

    partial_sums(2)
    is_self = same_home.astype(jnp.int32)
    tile_self = jnp.int32(0)
    for h in range(2):
        tile_self = tile_self + (tile_to(zl, h)[2]).astype(jnp.int32)
    inner = (bz > 0).astype(jnp.int32) + (bz < 2).astype(jnp.int32)
    pl.semaphore_wait(barrier, 5 + inner + 32 - is_self + 12 - tile_self)

    right_dev, left_dev = at(x_=x_right), at(x_=x_left)

    def ring(n, src, dst, device):
        return [
            remote(src.at[h], dst.at[h], x_send.at[n, h], x_recv.at[n, h], device) for h in range(2)
        ]

    sends = [
        ring(0, part.at[2, 0], half_in.at[0], right_dev),
        ring(1, part.at[2, 1], half_in.at[1], left_dev),
        ring(2, part.at[1, 1], from_side.at[0, 1], right_dev),
        ring(3, part.at[3, 0], from_side.at[1, 0], left_dev),
        ring(4, part.at[1, 0], from_side.at[0, 0], right_dev),
        ring(5, part.at[3, 1], from_side.at[1, 1], left_dev),
    ]
    for h in range(2):
        sends[0][h].start()
        sends[1][h].start()
    partial_sums(1)
    partial_sums(3)
    for h in range(2):
        sends[2][h].start()
        sends[3][h].start()
        sends[0][h].wait_recv()
        part[1, 0, h] = part[1, 0, h] + half_in[0, h]
        sends[4][h].start()
        sends[1][h].wait_recv()
        part[3, 1, h] = part[3, 1, h] + half_in[1, h]
        sends[5][h].start()
        if h == 0:
            partial_sums(0)
    for t in range(8):
        tables[t : t + 1, :] = jnp.cos(omega[...] * tau[t]) * tweight[t]

    load_v.wait()

    def split_v(n, carry):
        rows = pl.ds(pl.multiple_of(n * 64, 64), 64)
        high, low = halves(v_full[rows, :])
        v_high[rows, :] = high
        v_low[rows, :] = low
        return carry

    lax.fori_loop(0, 24, split_v, 0)

    cross = [
        remote(z_out.at[h], z_in.at[h], z_send.at[h], z_recv.at[h], at(zh_=other, zl_=5 - zl))
        for h in range(2)
    ]
    for h in range(2):
        for n in range(2, 6):
            sends[n][h].wait_recv()
        z_out[h] = part[0, other, h] + from_side[0, other, h] + from_side[1, other, h]
        cross[h].start()
        z_keep[h] = part[0, zh, h] + from_side[0, zh, h] + from_side[1, zh, h]

    member = zh * 4 + x
    mine = (zh * 4 + x_freq) * 4 + slot_freq
    table = tables[...]
    for h in range(2):
        cross[h].wait_recv()
        for t in range(8):
            green = [z_keep[h, v * 64 + t * 8 : v * 64 + t * 8 + 8, :] for v in range(2)]
            rest = [z_in[h, v * 64 + t * 8 : v * 64 + t * 8 + 8, :] for v in range(2)]
            times[t] = -2.0 * (green[0] + rest[0]) * (green[1] + rest[1])
        for k in range(32):
            total = table[0:1, k : k + 1] * times[0]
            for t in range(1, 8):
                total = total + table[t : t + 1, k : k + 1] * times[t]
            freqs[h, k] = total
        place = blocks.at[own, bx, lax.div(member, 2), pl.ds(pl.multiple_of(y * 16 + h * 8, 8), 8), :]

        def send_freq(n, carry, h=h, place=place):
            k = lax.rem(mine + n, 32)
            remote(freqs.at[h, k], place, a_send.at[h], a_recv.at[lax.div(member, 2)], freq_to(k)).start()
            return carry

        lax.fori_loop(1, 32, send_freq, 0)

        @pl.when(same_home)
        def _(h=h, place=place):
            pltpu.make_async_copy(freqs.at[h, mine], place, a_recv.at[lax.div(member, 2)]).start()

        @pl.when(jnp.logical_not(same_home))
        def _(h=h, place=place):
            remote(freqs.at[h, mine], place, a_self.at[h], a_recv.at[lax.div(member, 2)], freq_to(mine)).start()

    def expand(i, par, m2):
        m = 2 * m2 + par
        col = lax.rem(i + m, 12)
        here = pl.ds(pl.multiple_of(i * 128, 128), 128)
        there = pl.ds(pl.multiple_of(col * 128, 128), 128)
        value = blocks[i, par, m2]
        high, low = halves(value)
        p_high[here, there] = high
        p_low[here, there] = low

        @pl.when(m > 0)
        def _():
            high_t, low_t = halves(value.T)
            p_high[there, here] = high_t
            p_low[there, here] = low_t

    others = (bz, jnp.where(bz == 1, 0, 1), jnp.where(bz == 2, 0, 2))
    pair_devices = {"x": at(x_=x + 1 - 2 * bx), "y": at(y_=y + 1 - 2 * by)}
    middle = bz == 1
    up, down = 1, -1

    def quarter(q):
        return lax.rem(q + 2 * zh, 4)

    def source(piece, core):
        m2, ez, ex, ey = piece
        par = bx if ex == 0 else 1 - bx
        side = by if ey == 0 else 1 - by
        i = (side * 3 + others[ez]) * 2 + core
        small = jnp.logical_and(par == 0, side == 0)
        live = None if m2 % 2 == 0 else jnp.logical_or(quarter(m2) < 3, small)
        return i, par, live

    def guarded(live, action):
        if live is None:
            action()
        else:
            pl.when(live)(action)

    def copy_of(n, piece, lane, device):
        i, par, _live = source(piece, c)
        ref = blocks.at[i, par, quarter(piece[0])]
        return remote(ref, ref, g_send.at[lane, n], g_recv.at[n_of(piece)], device)

    def n_of(piece):
        m2, ez, ex, ey = piece
        par = bx if ex == 0 else 1 - bx
        side = by if ey == 0 else 1 - by
        return ((quarter(m2) * 2 + side) * 2 + par) * 3 + others[ez]

    def core_copy(piece, core):
        i, par, _live = source(piece, core)
        ref = blocks.at[i, par, quarter(piece[0])]
        n = n_of(piece)
        return remote(ref, ref, c_send.at[n], c_recv.at[n], at(c_=1 - c))

    def arrival(piece):
        m2, ez, ex, ey = piece
        moved = {"z": ez, "x": ex, "y": ey}
        return max((p for p, d in enumerate(SPREAD[m2]) if moved[d]), default=-1)

    def sends_of(n, piece):
        m2, ez, _ex, _ey = piece
        last = arrival(piece)
        found = []
        for axis in SPREAD[m2][last + 1 :]:
            if axis == "z":
                found.append((bz < 2, copy_of(n, piece, 0, neighbour(up))))
                found.append((bz > 0, copy_of(n, piece, 1, neighbour(down))))
            else:
                found.append((None, copy_of(n, piece, 2 if axis == "x" else 3, pair_devices[axis])))
        if last >= 0 and SPREAD[m2][last] == "z":
            lane, step = (0, up) if ez == 1 else (1, down)
            found.append((middle, copy_of(n, piece, lane, neighbour(step))))
        return found

    def pick(values, q):
        found = values[-1]
        for at_q in range(len(values) - 2, -1, -1):
            found = jnp.where(q == at_q, values[at_q], found)
        return found

    def unfold(batch, cores):
        def step(q, carry):
            index = quarter(pick([t[0] for t in batch], q))
            ex, ey = pick([t[2] for t in batch], q), pick([t[3] for t in batch], q)
            sz = pick([others[t[1]] for t in batch], q)
            theirs = pick(cores, q)
            par, side = bx + ex - 2 * bx * ex, by + ey - 2 * by * ey
            core = c + theirs - 2 * c * theirs
            i = (side * 3 + sz) * 2 + core

            @pl.when(jnp.logical_or(index < 3, jnp.logical_and(par == 0, side == 0)))
            def _():
                @pl.when(theirs == 1)
                def _():
                    ref = blocks.at[i, par, index]
                    n = ((index * 2 + side) * 2 + par) * 3 + sz
                    remote(ref, ref, c_send.at[n], c_recv.at[n], at(c_=1 - c)).wait_recv()

                expand(i, par, index)

            return carry

        lax.fori_loop(0, len(batch), step, 0)

    batches = [PIECES[n : n + BATCH] for n in range(0, len(PIECES), BATCH)]
    for b in range(len(batches) + 1):
        if b < len(batches):
            for q, piece in enumerate(batches[b]):
                _i, _par, live = source(piece, c)

                def take(n=b * BATCH + q, piece=piece):
                    if arrival(piece) >= 0:
                        copy_of(n, piece, 0, neighbour(up)).wait_recv()
                    for when, copy in sends_of(n, piece):
                        guarded(when, copy.start)
                    core_copy(piece, c).start()

                if arrival(piece) < 0:
                    ref = blocks.at[home, bx, quarter(piece[0])]
                    pltpu.make_async_copy(ref, ref, a_recv.at[quarter(piece[0])]).wait()
                guarded(live, take)
        mine_now = batches[b] if b < len(batches) else ()
        theirs_now = batches[b - 1] if b else ()
        unfold(mine_now + theirs_now, [0] * len(mine_now) + [1] * len(theirs_now))

    rows = pl.ds(pl.multiple_of(strip * 64, 64), 64)
    stack_a[:64, :] = v_high[rows, :]
    stack_a[64:, :] = v_low[rows, :]

    def product(src, high, low, use, start=0):
        def step(n, carry):
            n = lax.rem(n + start, 6)
            cols = pl.ds(pl.multiple_of(n * 256, 256), 256)
            both = dot(src[...], high[:, cols])
            use(n, cols, both[:64] + both[64:] + dot(src[:64, :], low[:, cols]))
            return carry

        lax.fori_loop(0, 6, step, 0)

    def keep(dst, cols, value):
        high, low = halves(value)
        dst[:64, cols] = high
        dst[64:, cols] = low

    def use_one(n, cols, value):
        first[:, cols] = value
        keep(stack_b, cols, value)

    def send_tile(n, cols, value):
        tiles[n] = value
        for h in range(2):
            q, slot, same = tile_to(n, h)
            src = tiles.at[n, pl.ds(32 * h, 32), :]
            dst = landed.at[slot_freq, slot]

            @pl.when(same)
            def _():
                pltpu.make_async_copy(src, dst, o_recv).start()

            @pl.when(jnp.logical_not(same))
            def _():
                remote(src, dst, o_send.at[2 * n + h], o_recv, at(x_=x_freq, y_=lax.div(q, 2), c_=lax.rem(q, 2), zl_=n)).start()

    product(stack_a, p_high, p_low, use_one)
    product(stack_b, v_high, v_low, lambda n, cols, value: keep(stack_a, cols, value))
    product(stack_a, p_high, p_low, lambda n, cols, value: keep(stack_b, cols, first[:, cols] + value))
    product(stack_b, v_high, v_low, send_tile, jnp.where(zl < 3, 3, 0))

    for h in range(2):
        for n in range(6):
            sends[n][h].wait_send()
        cross[h].wait_send()
        sent = freqs.at[h, pl.ds(0, 31)]
        pltpu.make_async_copy(sent, sent, a_send.at[h]).wait()

        @pl.when(jnp.logical_not(same_home))
        def _(h=h):
            pltpu.make_async_copy(freqs.at[h, 0], freqs.at[h, 0], a_self.at[h]).wait()

    for n, piece in enumerate(PIECES):
        _i, _par, live = source(piece, c)

        def drain(n=n, piece=piece):
            for when, copy in sends_of(n, piece):
                guarded(when, copy.wait_send)
            core_copy(piece, c).wait_send()

        guarded(live, drain)

    pltpu.make_async_copy(landed, landed, o_recv).wait()
    out[...] = landed[...].reshape(out.shape)

    def drain_tiles(n, carry):
        col, h = lax.div(n, 2), lax.rem(n, 2)
        same = tile_to(col, h)[2]

        @pl.when(jnp.logical_not(same))
        def _():
            src = tiles.at[0, pl.ds(0, 32), :]
            pltpu.make_async_copy(src, src, o_send.at[n]).wait()

        return carry

    lax.fori_loop(0, 12, drain_tiles, 0)


def on_device(c_occ, c_vir, eps_occ, eps_vir, tau, tweight, omega, coulomb):
    grid = coulomb.shape[0]
    width = c_occ.shape[1]
    dma = pltpu.SemaphoreType.DMA
    hbm = pl.BlockSpec(memory_space=pl.ANY)
    vmem, smem = pl.BlockSpec(memory_space=pltpu.VMEM), pl.BlockSpec(memory_space=pltpu.SMEM)
    return pl.pallas_call(
        kernel,
        out_shape=pltpu.VMEM((4, 96, 256), F32),
        in_specs=[smem, smem, vmem, vmem, vmem, hbm, hbm, hbm],
        out_specs=vmem,
        scratch_shapes=[
            pltpu.VMEM((128, width), F32),
            pltpu.VMEM((2, 256, width), BF16),
            pltpu.VMEM((4, 2, 2, 128, 128), F32),
            pltpu.VMEM((2, 2, 128, 128), F32),
            pltpu.VMEM((2, 2, 2, 128, 128), F32),
            pltpu.VMEM((2, 128, 128), F32),
            pltpu.VMEM((2, 128, 128), F32),
            pltpu.VMEM((2, 128, 128), F32),
            pltpu.VMEM((8, 8, 128), F32),
            pltpu.VMEM((2, 32, 8, 128), F32),
            pltpu.VMEM((12, 2, 4, 128, 128), F32),
            pltpu.VMEM((grid, grid), BF16),
            pltpu.VMEM((grid, grid), BF16),
            pltpu.VMEM((grid, grid), F32),
            pltpu.VMEM((grid, grid), BF16),
            pltpu.VMEM((grid, grid), BF16),
            pltpu.VMEM((64, grid), F32),
            pltpu.VMEM((128, grid), BF16),
            pltpu.VMEM((128, grid), BF16),
            pltpu.VMEM((6, 64, 256), F32),
            pltpu.VMEM((4, 3, 32, 256), F32),
            pltpu.VMEM((8, omega.shape[0]), F32),
            pltpu.VMEM((width, grid), F32),
            pltpu.VMEM((width, grid), F32),
            dma((2,)), dma, dma((6, 2)), dma((6, 2)), dma((2,)), dma((2,)), dma((2,)), dma((2,)), dma((4,)),
            dma((4, 48)), dma((48,)), dma((48,)), dma((48,)), dma((12,)), dma,
        ],
        compiler_params=pltpu.CompilerParams(
            collective_id=0, has_side_effects=True, vmem_limit_bytes=60 * 1024 * 1024
        ),
        name="screened",
    )(tau, tweight, omega[None, :], eps_occ[None, :], eps_vir[None, :], c_occ.T, c_vir.T, coulomb)


def solution(mesh):
    split = Mesh(mesh.devices.reshape(2, 4, 8, 2, 6), AXES)
    tm = ("zh", "x")
    placed = (P(None, tm), P(None, tm), P(tm), P(tm), P(), P(), P(), P())
    return jax.shard_map(
        on_device, mesh=split, in_specs=placed, out_specs=P(tm, ("y", "c"), "zl"), check_vma=False
    )
```

```python
import jax
import jax.numpy as jnp
from jax import lax
from jax.experimental import pallas as pl
from jax.experimental.pallas import tpu as pltpu
from jax.sharding import Mesh
from jax.sharding import PartitionSpec as P

AXES = ("zh", "x", "y", "c", "zl")
MESH_ID = pl.DeviceIdType.MESH
F32, BF16 = jnp.float32, jnp.bfloat16

BATCHES = (4,) * 11 + (2, 1, 1)
SPREAD = ("xzy", "yzx", "zxy", "yzx")
PIECES = (
    (0, 0, 0, 0), (1, 0, 0, 0), (0, 0, 1, 0), (2, 0, 0, 0), (3, 0, 0, 0), (1, 1, 0, 0),
    (1, 0, 1, 0), (1, 0, 0, 1), (2, 1, 0, 0), (0, 1, 1, 0), (1, 2, 0, 0), (3, 0, 0, 1),
    (3, 1, 0, 0), (0, 1, 0, 0), (2, 2, 0, 0), (1, 1, 0, 1), (2, 1, 0, 1), (0, 0, 0, 1),
    (2, 0, 1, 0), (0, 2, 1, 0), (0, 1, 1, 1), (0, 0, 1, 1), (3, 0, 1, 0), (3, 2, 0, 0),
    (1, 1, 1, 0), (1, 0, 1, 1), (0, 1, 0, 1), (3, 1, 0, 1), (0, 2, 0, 0), (1, 2, 1, 0),
    (2, 2, 0, 1), (2, 1, 1, 0), (1, 2, 0, 1), (2, 0, 1, 1), (3, 1, 1, 0), (3, 0, 1, 1),
    (1, 1, 1, 1), (0, 2, 1, 1), (3, 2, 0, 1), (2, 2, 1, 0), (3, 1, 1, 1), (0, 2, 0, 1),
    (2, 0, 0, 1), (3, 2, 1, 0), (2, 1, 1, 1), (1, 2, 1, 1), (3, 2, 1, 1), (2, 2, 1, 1),
)


def halves(value):
    high = value.astype(BF16)
    return high, (value - high.astype(F32)).astype(BF16)


def dot(a, b):
    return lax.dot_general(a, b, (((1,), (0,)), ((), ())), preferred_element_type=F32)


def remote(src, dst, send, recv, device):
    return pltpu.make_async_remote_copy(
        src_ref=src, dst_ref=dst, send_sem=send, recv_sem=recv, device_id=device, device_id_type=MESH_ID
    )


def kernel(
    tau, tweight, omega, eps_occ, eps_vir, occ_in, vir_in, coulomb, out,
    rows_t, left, part, half_in, from_side, z_out, z_in, z_keep, times, freqs, blocks,
    p_high, p_low, v_full, v_high, v_low, first, stack_a, stack_b, tiles, landed,
    tables, occ, vir, b_sem, v_sem, x_send, x_recv, z_send, z_recv, a_send, a_self, a_recv,
    g_send, g_recv, c_send, c_recv, o_send, o_recv,
):
    zh, x, y, c, zl = (lax.axis_index(a) for a in AXES)
    level = zl + zh * (5 - 2 * zl)
    own = level * 2 + c
    triple, bz = lax.div(level, 3), lax.rem(level, 3)
    x_pair, bx = lax.div(x, 2), lax.rem(x, 2)
    y_pair, by = lax.div(y, 2), lax.rem(y, 2)
    x_freq = 2 * x_pair + lax.rem(y_pair, 2)
    slot_freq = 2 * lax.div(y_pair, 2) + triple
    home = (by * 3 + bz) * 2 + c
    x_right, x_left = lax.rem(x + 1, 4), lax.rem(x + 3, 4)
    other = 1 - zh

    def at(zh_=zh, x_=x, y_=y, c_=c, zl_=zl):
        return (zh_, x_, y_, c_, zl_)

    def line_of(zh_, level_):
        return level_ + zh_ * (5 - 2 * level_)

    load_v = pltpu.make_async_copy(coulomb, v_full, v_sem)
    loads = [
        pltpu.make_async_copy(occ_in, occ, b_sem.at[0]),
        pltpu.make_async_copy(vir_in, vir, b_sem.at[1]),
    ]
    for load in loads:
        load.start()
    load_v.start()

    barrier = pltpu.get_barrier_semaphore()

    def greet(device):
        pl.semaphore_signal(barrier, inc=1, device_id=device, device_id_type=MESH_ID)

    strip = lax.rem(6 * (2 * by + bx) + c * 3 + bz + 6 * y_pair + 15, 24)

    def tile_to(col, h):
        half = 2 * strip + h
        q = lax.div(half, 3)
        same = jnp.logical_and(jnp.logical_and(q == 2 * y + c, col == zl), x_freq == x)
        return q, lax.rem(half, 3), same

    def tile_from(f, slot):
        y_pair_s = 2 * lax.div(f, 2) + bx
        r = lax.div(3 * (2 * y + c) + slot, 2)
        u = lax.rem(r + 81 - 6 * y_pair_s, 24)
        a, b = lax.div(u, 6), lax.rem(u, 6)
        x_s, y_s = 2 * x_pair + lax.rem(a, 2), 2 * y_pair_s + lax.div(a, 2)
        zl_s, c_s = line_of(zh, 3 * lax.rem(f, 2) + lax.rem(b, 3)), lax.div(b, 3)
        same = jnp.logical_and(
            jnp.logical_and(y_s == y, c_s == c), jnp.logical_and(zl_s == zl, x_s == x)
        )
        return at(x_=x_s, y_=y_s, c_=c_s, zl_=zl_s), same

    def freq_to(k):
        zh_k, x_k, f = lax.div(k, 16), lax.rem(lax.div(k, 4), 4), lax.rem(k, 4)
        x_d = 2 * lax.div(x_k, 2) + bx
        y_d = 2 * (2 * lax.div(f, 2) + lax.rem(x_k, 2)) + triple
        return (zh_k, x_d, y_d, c, line_of(zh_k, 3 * lax.rem(f, 2) + bz))

    greet(at(x_=x_left))
    greet(at(x_=x_right))
    greet(at(zh_=other, zl_=5 - zl))
    greet(at(y_=y + 1 - 2 * by))
    greet(at(c_=1 - c))

    def neighbour(step):
        return at(zl_=line_of(zh, level + step))

    @pl.when(bz > 0)
    def _():
        greet(neighbour(-1))

    @pl.when(bz < 2)
    def _():
        greet(neighbour(1))

    same_home = triple == by

    def greet_source(n, carry):
        zh_s, x_s, y_s = lax.div(n, 16), 2 * lax.rem(lax.div(n, 8), 2) + bx, lax.rem(n, 8)
        same = jnp.logical_and(jnp.logical_and(zh_s == zh, x_s == x), y_s == y)

        @pl.when(jnp.logical_not(jnp.logical_and(same, same_home)))
        def _():
            greet((zh_s, x_s, y_s, c, line_of(zh_s, by * 3 + bz)))

        return carry

    lax.fori_loop(0, 32, greet_source, 0)

    def greet_tile(n, carry):
        device, same = tile_from(lax.div(n, 3), lax.rem(n, 3))

        @pl.when(jnp.logical_not(same))
        def _():
            greet(device)

        return carry

    lax.fori_loop(0, 12, greet_tile, 0)

    for load in loads:
        load.wait()
    for side, (block, eps, sign) in enumerate(((occ, eps_occ, 1.0), (vir, eps_vir, -1.0))):
        rows_t[...] = block[:, pl.ds(pl.multiple_of(own * 128, 128), 128)].T
        rows = rows_t[pl.ds(pl.multiple_of(y * 16, 16), 16), :]
        for t in range(8):
            high, low = halves(rows * jnp.exp(eps[...] * (sign * tau[t])))
            for h in range(2):
                at_row = h * 64 + t * 8
                left[side, at_row : at_row + 8, :] = high[h * 8 : h * 8 + 8]
                left[side, 128 + at_row : 136 + at_row, :] = low[h * 8 : h * 8 + 8]

    def partial_sums(d):
        for z in range(2):
            col = lax.rem(own + z * 4 + lax.rem(x + d, 4), 12)
            for side, block in enumerate((occ, vir)):
                high, low = halves(block[:, pl.ds(pl.multiple_of(col * 128, 128), 128)])
                both = dot(left[side], high)
                whole = both[:128] + both[128:] + dot(left[side, :128, :], low)
                for h in range(2):
                    part[d, z, h, side * 64 : side * 64 + 64, :] = whole[h * 64 : h * 64 + 64]

    partial_sums(2)
    is_self = same_home.astype(jnp.int32)
    tile_self = jnp.int32(0)
    for h in range(2):
        tile_self = tile_self + (tile_to(zl, h)[2]).astype(jnp.int32)
    inner = (bz > 0).astype(jnp.int32) + (bz < 2).astype(jnp.int32)
    pl.semaphore_wait(barrier, 5 + inner + 32 - is_self + 12 - tile_self)

    right_dev, left_dev = at(x_=x_right), at(x_=x_left)

    def ring(n, src, dst, device):
        return [
            remote(src.at[h], dst.at[h], x_send.at[n, h], x_recv.at[n, h], device) for h in range(2)
        ]

    sends = [
        ring(0, part.at[2, 0], half_in.at[0], right_dev),
        ring(1, part.at[2, 1], half_in.at[1], left_dev),
        ring(2, part.at[1, 1], from_side.at[0, 1], right_dev),
        ring(3, part.at[3, 0], from_side.at[1, 0], left_dev),
        ring(4, part.at[1, 0], from_side.at[0, 0], right_dev),
        ring(5, part.at[3, 1], from_side.at[1, 1], left_dev),
    ]
    for h in range(2):
        sends[0][h].start()
        sends[1][h].start()
    partial_sums(1)
    partial_sums(3)
    for h in range(2):
        sends[2][h].start()
        sends[3][h].start()
        sends[0][h].wait_recv()
        part[1, 0, h] = part[1, 0, h] + half_in[0, h]
        sends[4][h].start()
        sends[1][h].wait_recv()
        part[3, 1, h] = part[3, 1, h] + half_in[1, h]
        sends[5][h].start()
        if h == 0:
            partial_sums(0)
    for t in range(8):
        tables[t : t + 1, :] = jnp.cos(omega[...] * tau[t]) * tweight[t]

    load_v.wait()

    def split_v(n, carry):
        rows = pl.ds(pl.multiple_of(n * 64, 64), 64)
        high, low = halves(v_full[rows, :])
        v_high[rows, :] = high
        v_low[rows, :] = low
        return carry

    lax.fori_loop(0, 24, split_v, 0)

    cross = [
        remote(z_out.at[h], z_in.at[h], z_send.at[h], z_recv.at[h], at(zh_=other, zl_=5 - zl))
        for h in range(2)
    ]
    for h in range(2):
        for n in range(2, 6):
            sends[n][h].wait_recv()
        z_out[h] = part[0, other, h] + from_side[0, other, h] + from_side[1, other, h]
        cross[h].start()
        z_keep[h] = part[0, zh, h] + from_side[0, zh, h] + from_side[1, zh, h]

    member = zh * 4 + x
    mine = (zh * 4 + x_freq) * 4 + slot_freq
    table = tables[...]
    for h in range(2):
        cross[h].wait_recv()
        for t in range(8):
            green = [z_keep[h, v * 64 + t * 8 : v * 64 + t * 8 + 8, :] for v in range(2)]
            rest = [z_in[h, v * 64 + t * 8 : v * 64 + t * 8 + 8, :] for v in range(2)]
            times[t] = -2.0 * (green[0] + rest[0]) * (green[1] + rest[1])
        for k in range(32):
            total = table[0:1, k : k + 1] * times[0]
            for t in range(1, 8):
                total = total + table[t : t + 1, k : k + 1] * times[t]
            freqs[h, k] = total
        place = blocks.at[own, bx, lax.div(member, 2), pl.ds(pl.multiple_of(y * 16 + h * 8, 8), 8), :]

        def send_freq(n, carry, h=h, place=place):
            k = lax.rem(mine + n, 32)
            remote(freqs.at[h, k], place, a_send.at[h], a_recv.at[lax.div(member, 2)], freq_to(k)).start()
            return carry

        lax.fori_loop(1, 32, send_freq, 0)

        @pl.when(same_home)
        def _(h=h, place=place):
            pltpu.make_async_copy(freqs.at[h, mine], place, a_recv.at[lax.div(member, 2)]).start()

        @pl.when(jnp.logical_not(same_home))
        def _(h=h, place=place):
            remote(freqs.at[h, mine], place, a_self.at[h], a_recv.at[lax.div(member, 2)], freq_to(mine)).start()

    def expand(i, par, m2):
        m = 2 * m2 + par
        col = lax.rem(i + m, 12)
        here = pl.ds(pl.multiple_of(i * 128, 128), 128)
        there = pl.ds(pl.multiple_of(col * 128, 128), 128)
        value = blocks[i, par, m2]
        high, low = halves(value)
        p_high[here, there] = high
        p_low[here, there] = low

        @pl.when(m > 0)
        def _():
            high_t, low_t = halves(value.T)
            p_high[there, here] = high_t
            p_low[there, here] = low_t

    others = (bz, jnp.where(bz == 1, 0, 1), jnp.where(bz == 2, 0, 2))
    pair_devices = {"x": at(x_=x + 1 - 2 * bx), "y": at(y_=y + 1 - 2 * by)}
    middle = bz == 1
    up, down = 1, -1

    def quarter(q):
        return lax.rem(q + 2 * zh, 4)

    def source(piece, core):
        m2, ez, ex, ey = piece
        par = bx if ex == 0 else 1 - bx
        side = by if ey == 0 else 1 - by
        i = (side * 3 + others[ez]) * 2 + core
        small = jnp.logical_and(par == 0, side == 0)
        live = None if m2 % 2 == 0 else jnp.logical_or(quarter(m2) < 3, small)
        return i, par, live

    def guarded(live, action):
        if live is None:
            action()
        else:
            pl.when(live)(action)

    def copy_of(n, piece, lane, device):
        i, par, _live = source(piece, c)
        ref = blocks.at[i, par, quarter(piece[0])]
        return remote(ref, ref, g_send.at[lane, n], g_recv.at[n_of(piece)], device)

    def n_of(piece):
        m2, ez, ex, ey = piece
        par = bx if ex == 0 else 1 - bx
        side = by if ey == 0 else 1 - by
        return ((quarter(m2) * 2 + side) * 2 + par) * 3 + others[ez]

    def core_copy(piece, core):
        i, par, _live = source(piece, core)
        ref = blocks.at[i, par, quarter(piece[0])]
        n = n_of(piece)
        return remote(ref, ref, c_send.at[n], c_recv.at[n], at(c_=1 - c))

    def arrival(piece):
        m2, ez, ex, ey = piece
        moved = {"z": ez, "x": ex, "y": ey}
        return max((p for p, d in enumerate(SPREAD[m2]) if moved[d]), default=-1)

    def sends_of(n, piece):
        m2, ez, _ex, _ey = piece
        last = arrival(piece)
        found = []
        for axis in SPREAD[m2][last + 1 :]:
            if axis == "z":
                found.append((bz < 2, copy_of(n, piece, 0, neighbour(up))))
                found.append((bz > 0, copy_of(n, piece, 1, neighbour(down))))
            else:
                found.append((None, copy_of(n, piece, 2 if axis == "x" else 3, pair_devices[axis])))
        if last >= 0 and SPREAD[m2][last] == "z":
            lane, step = (0, up) if ez == 1 else (1, down)
            found.append((middle, copy_of(n, piece, lane, neighbour(step))))
        return found

    def pick(values, q):
        found = values[-1]
        for at_q in range(len(values) - 2, -1, -1):
            found = jnp.where(q == at_q, values[at_q], found)
        return found

    def unfold(batch, cores):
        def step(q, carry):
            index = quarter(pick([t[0] for t in batch], q))
            ex, ey = pick([t[2] for t in batch], q), pick([t[3] for t in batch], q)
            sz = pick([others[t[1]] for t in batch], q)
            theirs = pick(cores, q)
            par, side = bx + ex - 2 * bx * ex, by + ey - 2 * by * ey
            core = c + theirs - 2 * c * theirs
            i = (side * 3 + sz) * 2 + core

            @pl.when(jnp.logical_or(index < 3, jnp.logical_and(par == 0, side == 0)))
            def _():
                @pl.when(theirs == 1)
                def _():
                    ref = blocks.at[i, par, index]
                    n = ((index * 2 + side) * 2 + par) * 3 + sz
                    remote(ref, ref, c_send.at[n], c_recv.at[n], at(c_=1 - c)).wait_recv()

                expand(i, par, index)

            return carry

        lax.fori_loop(0, len(batch), step, 0)

    starts = [sum(BATCHES[:b]) for b in range(len(BATCHES))]
    batches = [PIECES[n : n + size] for n, size in zip(starts, BATCHES)]
    for b in range(len(batches) + 1):
        if b < len(batches):
            for q, piece in enumerate(batches[b]):
                _i, _par, live = source(piece, c)

                def take(n=starts[b] + q, piece=piece):
                    if arrival(piece) >= 0:
                        copy_of(n, piece, 0, neighbour(up)).wait_recv()
                    for when, copy in sends_of(n, piece):
                        guarded(when, copy.start)
                    core_copy(piece, c).start()

                if arrival(piece) < 0:
                    ref = blocks.at[home, bx, quarter(piece[0])]
                    pltpu.make_async_copy(ref, ref, a_recv.at[quarter(piece[0])]).wait()
                guarded(live, take)
        mine_now = batches[b] if b < len(batches) else ()
        theirs_now = batches[b - 1] if b else ()
        unfold(mine_now + theirs_now, [0] * len(mine_now) + [1] * len(theirs_now))

    rows = pl.ds(pl.multiple_of(strip * 64, 64), 64)
    stack_a[:64, :] = v_high[rows, :]
    stack_a[64:, :] = v_low[rows, :]

    def product(src, high, low, use, start=0):
        def step(n, carry):
            n = lax.rem(n + start, 6)
            cols = pl.ds(pl.multiple_of(n * 256, 256), 256)
            both = dot(src[...], high[:, cols])
            use(n, cols, both[:64] + both[64:] + dot(src[:64, :], low[:, cols]))
            return carry

        lax.fori_loop(0, 6, step, 0)

    def keep(dst, cols, value):
        high, low = halves(value)
        dst[:64, cols] = high
        dst[64:, cols] = low

    def use_one(n, cols, value):
        first[:, cols] = value
        keep(stack_b, cols, value)

    def send_tile(n, cols, value):
        tiles[n] = value
        for h in range(2):
            q, slot, same = tile_to(n, h)
            src = tiles.at[n, pl.ds(32 * h, 32), :]
            dst = landed.at[slot_freq, slot]

            @pl.when(same)
            def _():
                pltpu.make_async_copy(src, dst, o_recv).start()

            @pl.when(jnp.logical_not(same))
            def _():
                remote(src, dst, o_send.at[2 * n + h], o_recv, at(x_=x_freq, y_=lax.div(q, 2), c_=lax.rem(q, 2), zl_=n)).start()

    product(stack_a, p_high, p_low, use_one)
    product(stack_b, v_high, v_low, lambda n, cols, value: keep(stack_a, cols, value))
    product(stack_a, p_high, p_low, lambda n, cols, value: keep(stack_b, cols, first[:, cols] + value))
    product(stack_b, v_high, v_low, send_tile, jnp.where(zl < 3, 3, 0))

    for h in range(2):
        for n in range(6):
            sends[n][h].wait_send()
        cross[h].wait_send()
        sent = freqs.at[h, pl.ds(0, 31)]
        pltpu.make_async_copy(sent, sent, a_send.at[h]).wait()

        @pl.when(jnp.logical_not(same_home))
        def _(h=h):
            pltpu.make_async_copy(freqs.at[h, 0], freqs.at[h, 0], a_self.at[h]).wait()

    for n, piece in enumerate(PIECES):
        _i, _par, live = source(piece, c)

        def drain(n=n, piece=piece):
            for when, copy in sends_of(n, piece):
                guarded(when, copy.wait_send)
            core_copy(piece, c).wait_send()

        guarded(live, drain)

    pltpu.make_async_copy(landed, landed, o_recv).wait()
    out[...] = landed[...].reshape(out.shape)

    def drain_tiles(n, carry):
        col, h = lax.div(n, 2), lax.rem(n, 2)
        same = tile_to(col, h)[2]

        @pl.when(jnp.logical_not(same))
        def _():
            src = tiles.at[0, pl.ds(0, 32), :]
            pltpu.make_async_copy(src, src, o_send.at[n]).wait()

        return carry

    lax.fori_loop(0, 12, drain_tiles, 0)


def on_device(c_occ, c_vir, eps_occ, eps_vir, tau, tweight, omega, coulomb):
    grid = coulomb.shape[0]
    width = c_occ.shape[1]
    dma = pltpu.SemaphoreType.DMA
    hbm = pl.BlockSpec(memory_space=pl.ANY)
    vmem, smem = pl.BlockSpec(memory_space=pltpu.VMEM), pl.BlockSpec(memory_space=pltpu.SMEM)
    return pl.pallas_call(
        kernel,
        out_shape=pltpu.VMEM((4, 96, 256), F32),
        in_specs=[smem, smem, vmem, vmem, vmem, hbm, hbm, hbm],
        out_specs=vmem,
        scratch_shapes=[
            pltpu.VMEM((128, width), F32),
            pltpu.VMEM((2, 256, width), BF16),
            pltpu.VMEM((4, 2, 2, 128, 128), F32),
            pltpu.VMEM((2, 2, 128, 128), F32),
            pltpu.VMEM((2, 2, 2, 128, 128), F32),
            pltpu.VMEM((2, 128, 128), F32),
            pltpu.VMEM((2, 128, 128), F32),
            pltpu.VMEM((2, 128, 128), F32),
            pltpu.VMEM((8, 8, 128), F32),
            pltpu.VMEM((2, 32, 8, 128), F32),
            pltpu.VMEM((12, 2, 4, 128, 128), F32),
            pltpu.VMEM((grid, grid), BF16),
            pltpu.VMEM((grid, grid), BF16),
            pltpu.VMEM((grid, grid), F32),
            pltpu.VMEM((grid, grid), BF16),
            pltpu.VMEM((grid, grid), BF16),
            pltpu.VMEM((64, grid), F32),
            pltpu.VMEM((128, grid), BF16),
            pltpu.VMEM((128, grid), BF16),
            pltpu.VMEM((6, 64, 256), F32),
            pltpu.VMEM((4, 3, 32, 256), F32),
            pltpu.VMEM((8, omega.shape[0]), F32),
            pltpu.VMEM((width, grid), F32),
            pltpu.VMEM((width, grid), F32),
            dma((2,)), dma, dma((6, 2)), dma((6, 2)), dma((2,)), dma((2,)), dma((2,)), dma((2,)), dma((4,)),
            dma((4, 48)), dma((48,)), dma((48,)), dma((48,)), dma((12,)), dma,
        ],
        compiler_params=pltpu.CompilerParams(
            collective_id=0, has_side_effects=True, vmem_limit_bytes=60 * 1024 * 1024
        ),
        name="screened",
    )(tau, tweight, omega[None, :], eps_occ[None, :], eps_vir[None, :], c_occ.T, c_vir.T, coulomb)


def solution(mesh):
    split = Mesh(mesh.devices.reshape(2, 4, 8, 2, 6), AXES)
    tm = ("zh", "x")
    placed = (P(None, tm), P(None, tm), P(tm), P(tm), P(), P(), P(), P())
    return jax.shard_map(
        on_device, mesh=split, in_specs=placed, out_specs=P(tm, ("y", "c"), "zl"), check_vma=False
    )
```
